256 devices in a mesh: ctx: 16 (over x_hi, y, core), head: 16 (over z, x_lo).
Axes of the slice: x: 4 (x_hi: 2, x_lo: 2; x = x_hi * 2 + x_lo), y: 4, z: 8, core: 2. Of those that a mesh axis runs over, the one named last changes fastest.
Arguments:
- queries: bfloat16 [32768, 2048], P(('ctx', 'head')), may hold values from -16 to 16
- keys: bfloat16 [32768, 512], P(('ctx', 'head')), may hold values from -4 to 4
- values: bfloat16 [32768, 512], P(('ctx', 'head')), may hold values from -6 to 6
- d_out: bfloat16 [32768, 2048], P(('ctx', 'head')), may hold values from -6 to 6
- lengths: int32 [32], replicated, may hold values from 1 to 8192, 32768 in all
Outputs:
- attn_out: bfloat16 [32768, 2048], P(('ctx', 'head'))
- grad_queries: bfloat16 [32768, 2048], P(('ctx', 'head'))
- grad_keys: bfloat16 [32768, 512], P(('ctx', 'head'))
- grad_values: bfloat16 [32768, 512], P(('ctx', 'head'))
The draws below stay inside these ranges and needn't reach their ends.
Inputs may be any that keep to these rules, and one draw needn't show every extreme that they name: The 32 lengths sum to 32768; the longest is exactly 8192.
All inputs are finite; a program needn't handle non-finite values.
Results may differ from the reference program's by a relative error of at most 0.035.
Values may be sent and summed in bfloat16 or wider, within the bound.
A program may use at most 128 MiB of HBM per device.

```python
import math
import jax
import jax.numpy as jnp
import numpy as np
from jax import lax

QH = 16
KVH = 4
HD = 128
DOCS = 32
SEQ = 32768
DOC_MOST = 8192


def key_field(key):
    return jnp.clip(jax.random.normal(jax.random.fold_in(key, 11), (SEQ, KVH * HD), jnp.float32), -4.0, 4.0)


def draw_keys(key, part):
    return key_field(key).astype(jnp.bfloat16)


def draw_queries(key, part):
    drawn = jnp.clip(jax.random.normal(jax.random.fold_in(key, 21), (SEQ, QH * HD), jnp.float32), -4.0, 4.0)
    return drawn.astype(jnp.bfloat16)


def shard_levels(rng, dims, pieces, least, top_value):
    def one(dim, parts):
        steps = jax.random.uniform(jax.random.fold_in(jax.random.fold_in(rng, 6), dim), (parts,), jnp.float32, least / len(pieces), top_value / len(pieces))
        return jnp.repeat(jnp.exp(steps), dims[dim] // parts).reshape((-1,) + (1,) * (len(dims) - dim - 1))

    factor_of = one(*pieces[0])
    for cut in pieces[1:]:
        factor_of = factor_of * one(*cut)
    return factor_of


def profile(amount, total, most, skew):
    weights = [(1 << 20) // math.isqrt(standing ** skew) + 1 for standing in range(2, amount + 1)]
    rest, counts = total - most - (amount - 1), [1] * (amount - 1)
    while rest > 0:
        candidates = [i for i in range(amount - 1) if counts[i] < most]
        whole, remaining = sum([weights[i] for i in candidates]), rest
        for i in candidates:
            addition = min(most - counts[i], max(1, remaining * weights[i] // whole), rest)
            counts[i] = counts[i] + addition
            rest = rest - addition
    return np.array([most] + counts)


def ragged_sizes(key, count, total, bound, skew):
    if count == 2:
        one = jax.random.randint(key, (), max(1, total - bound), min(bound, total - 1) + 1)
        return jnp.stack([one, total - one])
    sizes = jnp.asarray(profile(count, total, bound, skew), jnp.int32)
    pairs = (count - 1) // 2
    source_of, taker = sizes[1:1 + 2 * pairs:2], sizes[2:2 + 2 * pairs:2]
    margin = jnp.minimum(source_of - 1, bound - taker)
    passed = jax.random.randint(jax.random.fold_in(key, 1), (pairs,), 0, 1 << 20) % (margin + 1)
    sizes = sizes.at[1:1 + 2 * pairs:2].set(source_of - passed).at[2:2 + 2 * pairs:2].set(taker + passed)
    return sizes[jax.random.permutation(jax.random.fold_in(key, 2), count)]


def noise(stream_key, shape, width, most, pieces=(), kind=jnp.bfloat16):
    entries = width * jax.random.normal(stream_key, shape, jnp.float32)
    if pieces:
        entries = entries * shard_levels(stream_key, shape, pieces, -0.22, 0.18)
    return jnp.clip(entries, -most, most).astype(kind)


def setup_inputs(seed: int = 0) -> dict:
    arg_keys = jax.random.split(jax.random.key(seed), 6)
    return {
        "queries": draw_queries(jax.random.fold_in(arg_keys[5], 71), 0),
        "keys": draw_keys(jax.random.fold_in(arg_keys[5], 71), 0),
        "values": noise(arg_keys[2], (SEQ, KVH * HD), 1.0, 6.0, ((0, 256),)),
        "d_out": noise(arg_keys[3], (SEQ, QH * HD), 1.0, 6.0, ((0, 256),)),
        "lengths": ragged_sizes(arg_keys[4], DOCS, SEQ, DOC_MOST, 2).astype(jnp.int32),
    }


NEG_FILL = -1e30


def reference(queries, keys, values, d_out, lengths):
    total = queries.shape[0]
    group_size = QH // KVH
    scaling = HD ** -0.5
    block_rows = min(128, total)
    window = min(DOC_MOST + block_rows, total)
    doc_ends = jnp.cumsum(lengths)
    positions = jnp.arange(total, dtype=jnp.int32)
    starts = jnp.sum(jnp.where(doc_ends[None, :] <= positions[:, None], lengths[None, :], 0), axis=1).astype(jnp.int32)
    query_heads = queries.reshape(total, KVH, group_size, HD)
    key_heads = keys.reshape(total, KVH, HD)
    value_heads = values.reshape(total, KVH, HD)
    grad_heads = d_out.reshape(total, KVH, group_size, HD)

    def one_block(carried, block_index):
        key_acc, value_acc = carried
        first = block_index * block_rows
        window_first = jnp.clip(first + block_rows - window, 0, total - window).astype(jnp.int32)
        query_block = lax.dynamic_slice_in_dim(query_heads, first, block_rows, 0).astype(jnp.float32)
        grad_block = lax.dynamic_slice_in_dim(grad_heads, first, block_rows, 0).astype(jnp.float32)
        key_window = lax.dynamic_slice_in_dim(key_heads, window_first, window, 0).astype(jnp.float32)
        value_window = lax.dynamic_slice_in_dim(value_heads, window_first, window, 0).astype(jnp.float32)
        query_pos = first + jnp.arange(block_rows, dtype=jnp.int32)
        key_pos = window_first + jnp.arange(window, dtype=jnp.int32)
        start_rows = lax.dynamic_slice_in_dim(starts, first, block_rows, 0)
        mask = (key_pos[None, :] <= query_pos[:, None]) & (key_pos[None, :] >= start_rows[:, None])
        mask = mask[:, None, None, :]
        scores = jnp.einsum("qkgd,ckd->qkgc", query_block, key_window) * scaling
        masked = jnp.where(mask, scores, NEG_FILL)
        row_max = jnp.max(masked, axis=-1)
        row_total = jnp.sum(jnp.where(mask, jnp.exp(masked - row_max[..., None]), 0.0), axis=-1)
        lse_rows = row_max + jnp.log(row_total)
        prob_raw = jnp.where(mask, jnp.exp(scores - lse_rows[..., None]), 0.0)
        weights = lax.optimization_barrier(prob_raw.astype(jnp.bfloat16)).astype(jnp.float32)
        attn_block = jnp.einsum("qkgc,ckd->qkgd", weights, value_window).astype(jnp.bfloat16)
        delta_rows = jnp.sum(grad_block * attn_block.astype(jnp.float32), axis=-1)
        prob_grad = jnp.einsum("qkgd,ckd->qkgc", grad_block, value_window)
        score_grad = (prob_raw * (prob_grad - delta_rows[..., None]) * scaling).astype(jnp.bfloat16)
        score_grad = lax.optimization_barrier(score_grad).astype(jnp.float32)
        query_grad = jnp.einsum("qkgc,ckd->qkgd", score_grad, key_window).astype(jnp.bfloat16)
        key_part = jnp.einsum("qkgc,qkgd->ckd", score_grad, query_block)
        value_part = jnp.einsum("qkgc,qkgd->ckd", weights, grad_block)
        key_acc = lax.dynamic_update_slice_in_dim(key_acc, lax.dynamic_slice_in_dim(key_acc, window_first, window, 0) + key_part, window_first, 0)
        value_acc = lax.dynamic_update_slice_in_dim(value_acc, lax.dynamic_slice_in_dim(value_acc, window_first, window, 0) + value_part, window_first, 0)
        return (key_acc, value_acc), (attn_block, query_grad)

    empty = jnp.zeros((total, KVH, HD), jnp.float32)
    (key_acc, value_acc), (attn_blocks, query_grads) = lax.scan(one_block, (empty, empty), jnp.arange(total // block_rows, dtype=jnp.int32))
    attn_out = attn_blocks.reshape(total, QH * HD)
    grad_queries = query_grads.reshape(total, QH * HD)
    grad_keys = key_acc.reshape(total, KVH * HD).astype(jnp.bfloat16)
    grad_values = value_acc.reshape(total, KVH * HD).astype(jnp.bfloat16)
    return (attn_out, grad_queries, grad_keys, grad_values)
```

```python
import functools
import math

import jax
import jax.numpy as jnp
from jax import lax
from jax.experimental import pallas as pl
from jax.experimental.pallas import tpu as pltpu
from jax.sharding import PartitionSpec as P

QH = 16
KVH = 4
HD = 128
GROUP = QH // KVH
SEQ = 32768
DOC_MOST = 8192
NEG_FILL = -1e30

XHI, YN, ZN, XLO = 2, 4, 8, 2
RING = 32
HALF = 64
PIECES = XHI * YN
ROWS = GROUP * HALF
KB = 512
KBLOCKS = SEQ // KB
SPAN = DOC_MOST // KB + 2

MESH = pl.DeviceIdType.MESH
ANY = pl.BlockSpec(memory_space=pl.ANY)
VMEM = pl.BlockSpec(memory_space=pltpu.VMEM)
SMEM = pl.BlockSpec(memory_space=pltpu.SMEM)


def here():
    c = lax.axis_index("ctx")
    h = lax.axis_index("head")
    xh, y, core = c // 8, lax.rem(c // 2, 4), lax.rem(c, 2)
    z, xl = h // 2, lax.rem(h, 2)
    return xh * 2 + xl, y, z, core


def device(x, y, z, core):
    return ((x // 2) * 8 + y * 2 + core, z * 2 + lax.rem(x, 2))


def ring_place(ring, n):
    major, minor = n // 4, lax.rem(n, 4)
    if ring == 0:
        return lax.rem(minor + 3 * major, 4), major
    return lax.rem(major, 4), lax.rem(3 * major + minor, 8)


def ring_number(ring, x, z):
    if ring == 0:
        return 4 * z + lax.rem(x + z, 4)
    part = lax.rem(z + 5 * x, 8)
    return 4 * x + part + 12 * (part // 4)


def greet(peers):
    barrier = pltpu.get_barrier_semaphore()
    for peer in peers:
        pl.semaphore_signal(barrier, inc=1, device_id=peer, device_id_type=MESH)
    pl.semaphore_wait(barrier, len(peers))


def remote(src, dst, send, recv, peer):
    return pltpu.make_async_remote_copy(
        src_ref=src, dst_ref=dst, send_sem=send, recv_sem=recv, device_id=peer, device_id_type=MESH
    )


def lanes(start, size):
    return pl.ds(pl.multiple_of(start * size, size), size)


class Spot:
    def __init__(self):
        self.x, self.y, self.z, self.core = here()
        self.xh, self.xl = self.x // 2, lax.rem(self.x, 2)
        self.number = [ring_number(r, self.x, self.z) for r in range(2)]
        self.next = []
        for flow in range(4):
            ring, step = flow // 2, 1 if flow % 2 == 0 else RING - 1
            x, z = ring_place(ring, lax.rem(self.number[ring] + step, RING))
            self.next.append(device(x, self.y, z, self.core))
        self.partner = device(self.x, self.y, self.z, 1 - self.core)
        self.offsets = [(dx, dy) for dx in range(XHI) for dy in range(YN)]

    def part_of(self, dx, dy):
        return lax.rem(self.xh + dx, XHI), lax.rem(self.y + dy, YN)

    def part_device(self, dx, dy):
        xh, y = self.part_of(dx, dy)
        return device(xh * 2 + self.xl, y, self.z, self.core)

    def peers(self):
        return (
            self.next + [self.partner] + [self.part_device(dx, dy) for dx, dy in self.offsets[1:]]
        )

    def chunk(self, ref, ring, n, core):
        x, z = ring_place(ring, n)
        return ref.at[x // 2, :, core * 16 + z * 2 + lax.rem(x, 2)]


def gather_kernel(
    q_ref, k_ref, v_ref, g_ref, ka_ref, va_ref, qi_ref, gi_ref,
    y_send, y_recv, p_send, p_recv, r_send, r_recv, c_send, c_recv, local,
):
    at = Spot()
    greet(at.peers())
    mine = at.core * 16 + at.z * 2 + at.xl
    ours = [ka_ref, va_ref]
    copies = []
    for number, (src, dst) in enumerate([(k_ref, ka_ref), (v_ref, va_ref)]):
        keep = pltpu.make_async_copy(
            src.at[:, lanes(at.y, HD)], dst.at[at.xh, at.y, mine], local.at[number]
        )
        keep.start()
        copies.append(keep)
        for dy in range(1, YN):
            _, y = at.part_of(0, dy)
            send = remote(
                src.at[:, lanes(y, HD)],
                dst.at[at.xh, at.y, mine],
                y_send.at[number, dy],
                y_recv.at[number, dy],
                at.part_device(0, dy),
            )
            send.start()
            copies.append(send)
    for copy in copies:
        copy.wait()

    def forward(flow, step):
        ring = flow // 2
        if flow % 2 == 0:
            origin = lax.rem(at.number[ring] - step + RING, RING)
        else:
            origin = lax.rem(at.number[ring] + step, RING)
        piece = at.chunk(ours[ring], ring, origin, at.core)
        return remote(
            piece, piece, r_send.at[flow, step], r_recv.at[flow, step + 1], at.next[flow]
        )

    def across(flow, step):
        ring = flow // 2
        if flow % 2 == 0:
            origin = lax.rem(at.number[ring] - step + RING, RING)
        else:
            origin = lax.rem(at.number[ring] + step, RING)
        piece = at.chunk(ours[ring], ring, origin, at.core)
        return remote(piece, piece, c_send.at[flow, step], c_recv.at[flow, step], at.partner)

    def arrived(flow, step):
        forward(flow, step - 1).wait_recv()

    for flow in range(4):
        forward(flow, 0).start()
    for flow in (0, 2):
        across(flow, 0).start()
    moves = []
    for number, (src, dst) in enumerate([(q_ref, qi_ref), (g_ref, gi_ref)]):
        for place, (dx, dy) in enumerate(at.offsets):
            xh, y = at.part_of(dx, dy)
            piece = src.at[pl.ds(pl.multiple_of(xh * HALF, HALF), HALF), lanes(y, GROUP * HD)]
            slot = dst.at[at.xh * YN + at.y]
            if place == 0:
                move = pltpu.make_async_copy(piece, slot, local.at[2 + number])
            else:
                move = remote(
                    piece,
                    slot,
                    p_send.at[number, place],
                    p_recv.at[number, place],
                    at.part_device(dx, dy),
                )
            move.start()
            moves.append(move)

    def step_body(step, carry):
        for flow in range(4):
            arrived(flow, step)
            forward(flow, step).start()
            across(flow, step).start()
        return carry

    lax.fori_loop(1, 15, step_body, 0)
    for flow in range(4):
        arrived(flow, 15)
        if flow % 2 == 0:
            forward(flow, 15).start()
        across(flow, 15).start()
    for flow in (0, 2):
        arrived(flow, 16)
        across(flow, 16).start()
    for move in moves:
        move.wait()

    def drain(step, carry):
        for flow in range(4):
            forward(flow, step).wait_send()
            across(flow, step).wait()
        return carry

    for flow in range(4):
        forward(flow, 0).wait_send()
    lax.fori_loop(1, 15, drain, 0)
    for flow in range(4):
        across(flow, 15).wait()
    for flow in (0, 2):
        forward(flow, 15).wait_send()
        across(flow, 0).wait()
        across(flow, 16).wait()


def gather(queries, keys, values, d_out):
    whole = jax.ShapeDtypeStruct((XHI, YN, 32, 128, HD), jnp.bfloat16)
    part = jax.ShapeDtypeStruct((PIECES, HALF, GROUP * HD), jnp.bfloat16)
    dma = pltpu.SemaphoreType.DMA
    return pl.pallas_call(
        gather_kernel,
        out_shape=(whole, whole, part, part),
        in_specs=[ANY] * 4,
        out_specs=(ANY,) * 4,
        scratch_shapes=[
            dma((2, YN)), dma((2, YN)), dma((2, PIECES)), dma((2, PIECES)),
            dma((4, 17)), dma((4, 17)), dma((4, 17)), dma((4, 17)), dma((4,)),
        ],
        compiler_params=pltpu.CompilerParams(collective_id=0, has_side_effects=True),
        name="gather",
    )(queries, keys, values, d_out)


def attention_kernel(
    meta, touched, start_ref, q_ref, g_ref, ka_ref, va_ref, o_ref, dq_ref, dk_ref, dv_ref,
    kbuf, vbuf, sbuf, pbuf, dk_acc, dv_acc, flush, k_sem, v_sem, f_sem,
):
    scaling = HD ** (-0.5)
    factor = scaling * math.log2(math.e)

    def rows_of(j):
        return pl.ds(pl.multiple_of(j * KB, KB), KB)

    def fetches(i, slot, j):
        src = rows_of(meta[i, 0] + j)
        return (
            pltpu.make_async_copy(ka_ref.at[src], kbuf.at[slot, rows_of(j)], k_sem.at[slot, j]),
            pltpu.make_async_copy(va_ref.at[src], vbuf.at[slot, rows_of(j)], v_sem.at[slot, j]),
        )

    def fetch(i, slot):
        def body(j, carry):
            for copy in fetches(i, slot, j):
                copy.start()
            return carry

        lax.fori_loop(0, meta[i, 1], body, 0)

    def stacked(value):
        return jnp.concatenate([value[:, h * HD : (h + 1) * HD] for h in range(GROUP)], axis=0)

    def unstacked(value):
        return jnp.concatenate([value[h * HALF : (h + 1) * HALF] for h in range(GROUP)], axis=1)

    def mm(a, b, da, db):
        return lax.dot_general(
            a, b, (((da,), (db,)), ((), ())), preferred_element_type=jnp.float32
        )

    fetch(0, 0)

    def piece(i, seen):
        slot = lax.rem(i, 2)

        @pl.when(i + 1 < PIECES)
        def _():
            fetch(i + 1, 1 - slot)

        low, count, first = meta[i, 0], meta[i, 1], meta[i, 2]
        q = stacked(q_ref[i])
        g = stacked(g_ref[i])
        starts = start_ref[i]
        times = first + lax.rem(lax.broadcasted_iota(jnp.int32, (1, ROWS), 1), HALF)
        key_iota = lax.broadcasted_iota(jnp.int32, (KB, ROWS), 0)

        def scores_step(j, top):
            fetches(i, slot, j)[0].wait()
            s = mm(kbuf[slot, rows_of(j)], q, 1, 1)
            base = (low + j) * KB
            s = jnp.where((key_iota >= starts - base) & (key_iota <= times - base), s, NEG_FILL)
            sbuf[rows_of(j)] = s
            return jnp.maximum(top, jnp.max(s.reshape(KB // 8, 8, ROWS), axis=0))

        top = lax.fori_loop(0, count, scores_step, jnp.full((8, ROWS), NEG_FILL, jnp.float32))
        top = jnp.max(top, axis=0, keepdims=True)

        def weights_step(j, carry):
            total, out = carry
            fetches(i, slot, j)[1].wait()
            p = jnp.exp2((sbuf[rows_of(j)] - top) * factor)
            total = total + jnp.sum(p.reshape(KB // 8, 8, ROWS), axis=0)
            p = p.astype(jnp.bfloat16)
            pbuf[rows_of(j)] = p
            return total, out + mm(vbuf[slot, rows_of(j)], p, 0, 0)

        total, out = lax.fori_loop(
            0,
            count,
            weights_step,
            (jnp.zeros((8, ROWS), jnp.float32), jnp.zeros((HD, ROWS), jnp.float32)),
        )
        inverse = 1.0 / jnp.sum(total, axis=0, keepdims=True)
        out = (out * inverse).astype(jnp.bfloat16).astype(jnp.float32)
        o_ref[i] = unstacked(out.T.astype(jnp.bfloat16))
        g_turned = g.astype(jnp.float32).T
        delta = jnp.sum(g_turned * out, axis=0, keepdims=True) * inverse
        g_turned = g_turned * inverse
        g_rows = g_turned.T.astype(jnp.bfloat16)

        def clear(kb, carry):
            dk_acc[rows_of(kb)] = jnp.zeros((KB, HD), jnp.float32)
            dv_acc[rows_of(kb)] = jnp.zeros((KB, HD), jnp.float32)
            return carry

        lax.fori_loop(jnp.maximum(low, seen), low + count, clear, 0)

        def grad_step(j, dq):
            k = kbuf[slot, rows_of(j)]
            p = pbuf[rows_of(j)]
            gp = mm(vbuf[slot, rows_of(j)], g_rows, 1, 1)
            ds = (p.astype(jnp.float32) * (gp - delta)).astype(jnp.bfloat16)
            where = rows_of(low + j)
            dv_acc[where] += mm(p, g_rows, 1, 0)
            dk_acc[where] += mm(ds, q, 1, 0)
            return dq + mm(k, ds, 0, 0)

        dq = lax.fori_loop(0, count, grad_step, jnp.zeros((HD, ROWS), jnp.float32))
        dq_ref[i] = unstacked((dq * scaling).T.astype(jnp.bfloat16))
        return low + count

    lax.fori_loop(0, PIECES, piece, 0)

    def flushes(kb, slot):
        return (
            pltpu.make_async_copy(flush.at[0, slot], dk_ref.at[rows_of(kb)], f_sem.at[0, slot]),
            pltpu.make_async_copy(flush.at[1, slot], dv_ref.at[rows_of(kb)], f_sem.at[1, slot]),
        )

    def flush_step(kb, carry):
        slot = lax.rem(kb, 2)

        @pl.when(kb >= 2)
        def _():
            for copy in flushes(kb - 2, slot):
                copy.wait()

        @pl.when(touched[kb] > 0)
        def _():
            flush[0, slot] = (dk_acc[rows_of(kb)] * scaling).astype(jnp.bfloat16)
            flush[1, slot] = dv_acc[rows_of(kb)].astype(jnp.bfloat16)

        @pl.when(touched[kb] == 0)
        def _():
            flush[0, slot] = jnp.zeros((KB, HD), jnp.bfloat16)
            flush[1, slot] = jnp.zeros((KB, HD), jnp.bfloat16)

        for copy in flushes(kb, slot):
            copy.start()
        return carry

    lax.fori_loop(0, KBLOCKS, flush_step, 0)
    for kb in (KBLOCKS - 2, KBLOCKS - 1):
        for copy in flushes(kb, kb % 2):
            copy.wait()


def attention(lengths, q, g, keys, values):
    x, y, z, core = here()
    ends = jnp.cumsum(lengths)
    part = jnp.arange(PIECES, dtype=jnp.int32)
    block = (part // YN) * 128 + lax.rem(part, YN) * 32 + core * 16 + z * 2 + lax.rem(x, 2)
    first = block * 128 + (x // 2) * HALF
    times = first[:, None] + jnp.arange(HALF, dtype=jnp.int32)[None, :]
    starts = jnp.sum(
        jnp.where(ends[None, None, :] <= times[:, :, None], lengths[None, None, :], 0), axis=2
    )
    low = starts[:, 0] // KB
    high = (first + HALF - 1) // KB
    meta = jnp.stack([low, high - low + 1, first], axis=1).astype(jnp.int32)
    block_ids = jnp.arange(KBLOCKS, dtype=jnp.int32)[:, None]
    touched = jnp.any((block_ids >= low[None]) & (block_ids <= high[None]), axis=1)
    start_rows = jnp.tile(starts, (1, GROUP)).reshape(PIECES, 1, ROWS).astype(jnp.int32)
    part_shape = jax.ShapeDtypeStruct((PIECES, HALF, GROUP * HD), jnp.bfloat16)
    whole = jax.ShapeDtypeStruct((SEQ, HD), jnp.bfloat16)
    dma = pltpu.SemaphoreType.DMA
    return pl.pallas_call(
        attention_kernel,
        out_shape=(part_shape, part_shape, whole, whole),
        in_specs=[SMEM, SMEM, VMEM, VMEM, VMEM, ANY, ANY],
        out_specs=(VMEM, VMEM, ANY, ANY),
        scratch_shapes=[
            pltpu.VMEM((2, SPAN * KB, HD), jnp.bfloat16),
            pltpu.VMEM((2, SPAN * KB, HD), jnp.bfloat16),
            pltpu.VMEM((SPAN * KB, ROWS), jnp.float32),
            pltpu.VMEM((SPAN * KB, ROWS), jnp.bfloat16),
            pltpu.VMEM((SEQ, HD), jnp.float32),
            pltpu.VMEM((SEQ, HD), jnp.float32),
            pltpu.VMEM((2, 2, KB, HD), jnp.bfloat16),
            dma((2, SPAN)),
            dma((2, SPAN)),
            dma((2, 2)),
        ],
        compiler_params=pltpu.CompilerParams(vmem_limit_bytes=62 << 20),
        name="attention",
    )(
        meta,
        touched.astype(jnp.int32),
        start_rows,
        q,
        g,
        keys.reshape(SEQ, HD),
        values.reshape(SEQ, HD),
    )


def scatter_kernel(
    o_ref, dq_ref, dk_ref, dv_ref, ao_ref, gq_ref, gk_ref, gv_ref,
    own, part, recv, done,
    own_sem, c_send, c_recv, r_send, r_recv, p_send, p_recv, y_send, y_recv, local,
):
    at = Spot()
    greet(at.peers())
    ours = [dk_ref, dv_ref]

    def target(flow, step):
        ring = flow // 2
        if flow % 2 == 0:
            return lax.rem(at.number[ring] + 17 - step, RING)
        return lax.rem(at.number[ring] + 16 + step, RING)

    def load(flow, step, n):
        piece = at.chunk(ours[flow // 2], flow // 2, n, at.core)
        return pltpu.make_async_copy(piece, own.at[flow, step], own_sem.at[flow, step])

    def across(flow, step, n):
        piece = at.chunk(ours[flow // 2], flow // 2, n, 1 - at.core)
        return remote(
            piece, part.at[flow, step], c_send.at[flow, step], c_recv.at[flow, step], at.partner
        )

    def forward(flow, step):
        return remote(
            own.at[flow, step],
            recv.at[flow, step - 1],
            r_send.at[flow, step - 1],
            r_recv.at[flow, step - 1],
            at.next[flow],
        )

    def begin(step, carry):
        for flow in range(4):
            load(flow, step, target(flow, step)).start()
            across(flow, step, target(flow, step)).start()
        return carry

    lax.fori_loop(1, 16, begin, 0)
    for flow in (0, 2):
        load(flow, 16, target(flow, 16)).start()
        across(flow, 16, target(flow, 16)).start()
        load(flow, 0, at.number[flow // 2]).start()
        across(flow, 0, at.number[flow // 2]).start()
    moves = []
    for number, (src, dst) in enumerate([(o_ref, ao_ref), (dq_ref, gq_ref)]):
        for place, (dx, dy) in enumerate(at.offsets):
            xh, y = at.part_of(dx, dy)
            piece = src.at[xh * YN + y]
            slot = dst.at[
                pl.ds(pl.multiple_of(at.xh * HALF, HALF), HALF), lanes(at.y, GROUP * HD)
            ]
            if place == 0:
                move = pltpu.make_async_copy(piece, slot, local.at[number])
            else:
                move = remote(
                    piece,
                    slot,
                    p_send.at[number, place],
                    p_recv.at[number, place],
                    at.part_device(dx, dy),
                )
            move.start()
            moves.append(move)

    def wide(ref, flow, step):
        return ref[flow, step].astype(jnp.float32)

    def ready(flow, step, n):
        load(flow, step, n).wait()
        across(flow, step, n).wait_recv()

    def send(flow, step, first):
        ready(flow, step, target(flow, step))
        total = wide(own, flow, step) + wide(part, flow, step)
        if not first:
            forward(flow, step - 1).wait_recv()
            total = total + wide(recv, flow, step - 2)
        own[flow, step] = total.astype(jnp.bfloat16)
        forward(flow, step).start()

    for flow in range(4):
        send(flow, 1, True)

    def step_body(step, carry):
        for flow in range(4):
            send(flow, step, False)
        return carry

    lax.fori_loop(2, 16, step_body, 0)
    for flow in (0, 2):
        send(flow, 16, False)
    for number, flow in enumerate((0, 2)):
        ready(flow, 0, at.number[number])
        total = wide(own, flow, 0) + wide(part, flow, 0)
        forward(flow, 16).wait_recv()
        forward(flow + 1, 15).wait_recv()
        total = total + wide(recv, flow, 15) + wide(recv, flow + 1, 14)
        done[number] = total.astype(jnp.bfloat16)
        dst = (gk_ref, gv_ref)[number]
        for dy in range(YN):
            _, y = at.part_of(0, dy)
            slot = dst.at[:, lanes(at.y, HD)]
            if dy == 0:
                move = pltpu.make_async_copy(done.at[number, y], slot, local.at[2 + number])
            else:
                move = remote(
                    done.at[number, y],
                    slot,
                    y_send.at[number, dy],
                    y_recv.at[number, dy],
                    at.part_device(0, dy),
                )
            move.start()
            moves.append(move)
    for move in moves:
        move.wait()

    def drain(step, carry):
        for flow in range(4):
            forward(flow, step).wait_send()
            across(flow, step, target(flow, step)).wait_send()
        return carry

    lax.fori_loop(1, 16, drain, 0)
    for flow in (0, 2):
        forward(flow, 16).wait_send()
        across(flow, 16, target(flow, 16)).wait_send()
        across(flow, 0, at.number[flow // 2]).wait_send()


def scatter(out, dq, dk, dv):
    tokens = jax.ShapeDtypeStruct((128, QH * HD), jnp.bfloat16)
    pairs = jax.ShapeDtypeStruct((128, KVH * HD), jnp.bfloat16)
    dma = pltpu.SemaphoreType.DMA
    slots = (YN, 128, HD)
    return pl.pallas_call(
        scatter_kernel,
        out_shape=(tokens, tokens, pairs, pairs),
        in_specs=[ANY] * 4,
        out_specs=(ANY,) * 4,
        scratch_shapes=[
            pltpu.VMEM((4, 17) + slots, jnp.bfloat16),
            pltpu.VMEM((4, 17) + slots, jnp.bfloat16),
            pltpu.VMEM((4, 16) + slots, jnp.bfloat16),
            pltpu.VMEM((2,) + slots, jnp.bfloat16),
            dma((4, 17)), dma((4, 17)), dma((4, 17)), dma((4, 16)), dma((4, 16)),
            dma((2, PIECES)), dma((2, PIECES)), dma((2, YN)), dma((2, YN)), dma((4,)),
        ],
        compiler_params=pltpu.CompilerParams(
            collective_id=1, has_side_effects=True, vmem_limit_bytes=48 << 20
        ),
        name="scatter",
    )(
        out,
        dq,
        dk.reshape(XHI, YN, 32, 128, HD),
        dv.reshape(XHI, YN, 32, 128, HD),
    )


def shards(queries, keys, values, d_out, lengths):
    ka, va, q, g = gather(queries, keys, values, d_out)
    out, dq, dk, dv = attention(lengths, q, g, ka, va)
    return scatter(out, dq, dk, dv)


def solution(mesh):
    spec = P(("ctx", "head"), None)
    return jax.shard_map(
        shards,
        mesh=mesh,
        in_specs=(spec, spec, spec, spec, P()),
        out_specs=(spec,) * 4,
        check_vma=False,
    )
```

```python
import functools
import math

import jax
import jax.numpy as jnp
from jax import lax
from jax.experimental import pallas as pl
from jax.experimental.pallas import tpu as pltpu
from jax.sharding import PartitionSpec as P

QH = 16
KVH = 4
HD = 128
GROUP = QH // KVH
SEQ = 32768
DOC_MOST = 8192
NEG_FILL = -1e30

XHI, XN, YN, ZN, XLO = 2, 4, 4, 8, 2
WHOLE = (XHI, YN, 2, ZN, XLO, 128, 128)
HALF = 64
PIECES = XHI * YN
ROWS = GROUP * HALF
KB = 512
KBLOCKS = SEQ // KB
SPAN = DOC_MOST // KB + 2

MESH = pl.DeviceIdType.MESH
ANY = pl.BlockSpec(memory_space=pl.ANY)
VMEM = pl.BlockSpec(memory_space=pltpu.VMEM)
SMEM = pl.BlockSpec(memory_space=pltpu.SMEM)


def here():
    c = lax.axis_index("ctx")
    h = lax.axis_index("head")
    xh, y, core = c // 8, lax.rem(c // 2, 4), lax.rem(c, 2)
    z, xl = h // 2, lax.rem(h, 2)
    return xh * 2 + xl, y, z, core


def device(x, y, z, core):
    return ((x // 2) * 8 + y * 2 + core, z * 2 + lax.rem(x, 2))


def greet(peers):
    barrier = pltpu.get_barrier_semaphore()
    for peer in peers:
        pl.semaphore_signal(barrier, inc=1, device_id=peer, device_id_type=MESH)
    pl.semaphore_wait(barrier, len(peers))


def remote(src, dst, send, recv, peer):
    return pltpu.make_async_remote_copy(
        src_ref=src, dst_ref=dst, send_sem=send, recv_sem=recv, device_id=peer, device_id_type=MESH
    )


def lanes(start, size):
    return pl.ds(pl.multiple_of(start * size, size), size)


class Spot:
    def __init__(self):
        self.x, self.y, self.z, self.core = here()
        self.xh, self.xl = self.x // 2, lax.rem(self.x, 2)
        self.x_peer = [device(self.x_at(d), self.y, self.z, self.core) for d in (1, -1)]
        self.z_peer = [device(self.x, self.y, self.z_at(d), self.core) for d in (1, -1)]
        self.partner = device(self.x, self.y, self.z, 1 - self.core)
        self.offsets = [(dx, dy) for dx in range(XHI) for dy in range(YN)]

    def x_at(self, d):
        return lax.rem(self.x + d + XN, XN)

    def z_at(self, d):
        return lax.rem(self.z + d + ZN, ZN)

    def part_of(self, dx, dy):
        return lax.rem(self.xh + dx, XHI), lax.rem(self.y + dy, YN)

    def part_device(self, dx, dy):
        xh, y = self.part_of(dx, dy)
        return device(xh * 2 + self.xl, y, self.z, self.core)

    def peers(self):
        return (
            self.x_peer
            + self.z_peer
            + [self.partner]
            + [self.part_device(dx, dy) for dx, dy in self.offsets[1:]]
        )

    def across_x(self, ref, core, dz, half=None):
        return ref.at[:, halves(half), core, self.z_at(dz)]

    def chunk(self, ref, dx, dz, half=None):
        x = self.x_at(dx)
        return ref.at[x // 2, halves(half), self.core, self.z_at(dz), lax.rem(x, 2)]


def halves(half):
    return pl.ds(0, YN) if half is None else pl.ds(half * 2, 2)


def gather_kernel(
    q_ref, k_ref, v_ref, g_ref, ka_ref, va_ref, qi_ref, gi_ref,
    y_send, y_recv, p_send, p_recv, kx_send, kx_recv, kz_send, kz_recv, vz_send, vz_recv,
    vx_send, vx_recv, c_send, c_recv, local,
):
    at = Spot()
    greet(at.peers())
    copies = []
    for number, (src, dst) in enumerate([(v_ref, va_ref), (k_ref, ka_ref)]):
        slot = dst.at[at.xh, at.y, at.core, at.z, at.xl]
        keep = pltpu.make_async_copy(src.at[:, lanes(at.y, HD)], slot, local.at[number])
        keep.start()
        copies.append([keep])
        for dy in range(1, YN):
            _, y = at.part_of(0, dy)
            send = remote(
                src.at[:, lanes(y, HD)],
                slot,
                y_send.at[number, dy],
                y_recv.at[number, dy],
                at.part_device(0, dy),
            )
            send.start()
            copies[number].append(send)

    sent, crossing = [], []

    def go(piece, send, recv, peer):
        copy = remote(piece, piece, send, recv, peer)
        copy.start()
        sent.append(copy)
        return copy

    def cross(piece):
        number = len(crossing)
        crossing.append(go(piece, c_send.at[number], c_recv.at[number], at.partner))

    def kx(number, piece, way):
        return go(piece, kx_send.at[number], kx_recv.at[number], at.x_peer[way])

    def kz(step, half, way):
        dz = (1 - step) if way == 0 else (step - 1)
        piece = at.across_x(ka_ref, at.core, dz, half)
        place = (way, step, half)
        return go(piece, kz_send.at[place], kz_recv.at[place], at.z_peer[way])

    def vz(step, way):
        dz = (1 - step) if way == 0 else (step - 1)
        piece = at.chunk(va_ref, 0, dz, way if step == 4 else None)
        return go(piece, vz_send.at[way, step], vz_recv.at[way, step], at.z_peer[way])

    vx_first, vx_second = {}, {}

    def vx(stage, way, dz, piece):
        place = (stage, way, dz + 3)
        return go(piece, vx_send.at[place], vx_recv.at[place], at.x_peer[way])

    def vx_start(dz):
        vx_first[dz] = [vx(0, way, dz, at.chunk(va_ref, 0, dz)) for way in range(2)]

    def vx_forward(dz):
        vx_second[dz] = []
        for way in range(2):
            vx_first[dz][way].wait_recv()
            piece = at.chunk(va_ref, 2 * way - 1, dz, way)
            vx_second[dz].append(vx(1, way, dz, piece))

    def vx_end(dz):
        for copy in vx_second[dz]:
            copy.wait_recv()
        cross(at.across_x(va_ref, at.core, dz))

    def kz_step(before, step):
        after = {}
        for half in range(2):
            for way in range(2):
                if (half, way) not in before:
                    continue
                before[half, way].wait_recv()
                if step < 4 or (step == 4 and half == way):
                    after[half, way] = kz(step, half, way)
                dz = (1 - step) if way == 0 else (step - 1)
                cross(at.across_x(ka_ref, at.core, dz, half))
        return after

    for copy in copies[0]:
        copy.wait()
    v_step = [vz(1, way) for way in range(2)]
    vx_start(0)
    for copy in copies[1]:
        copy.wait()
    k_first = [kx(way, at.chunk(ka_ref, 0, 0), way) for way in range(2)]

    moves = []
    for number, (src, dst) in enumerate([(q_ref, qi_ref), (g_ref, gi_ref)]):
        for place, (dx, dy) in enumerate(at.offsets):
            xh, y = at.part_of(dx, dy)
            piece = src.at[pl.ds(pl.multiple_of(xh * HALF, HALF), HALF), lanes(y, GROUP * HD)]
            slot = dst.at[at.xh * YN + at.y]
            if place == 0:
                move = pltpu.make_async_copy(piece, slot, local.at[2 + number])
            else:
                move = remote(
                    piece,
                    slot,
                    p_send.at[number, place],
                    p_recv.at[number, place],
                    at.part_device(dx, dy),
                )
            move.start()
            moves.append(move)

    k_second = []
    for way in range(2):
        k_first[way].wait_recv()
        k_second.append(kx(2 + way, at.chunk(ka_ref, 2 * way - 1, 0, way), way))

    def vz_next(step):
        for way in range(2):
            v_step[way].wait_recv()
            v_step[way] = vz(step, way)
            vx_start((1 - step) if way == 0 else (step - 1))

    vz_next(2)
    for copy in k_second:
        copy.wait_recv()
    k_step = {(half, way): kz(1, half, way) for half in range(2) for way in range(2)}
    cross(at.across_x(ka_ref, at.core, 0))
    vz_next(3)
    vx_forward(0)
    vz_next(4)
    vx_forward(-1)
    vx_forward(1)
    vx_end(0)
    for way in range(2):
        v_step[way].wait_recv()
    vx_start(4)
    k_step = kz_step(k_step, 2)
    vx_forward(-2)
    vx_forward(2)
    vx_end(-1)
    vx_end(1)
    k_step = kz_step(k_step, 3)
    vx_forward(-3)
    vx_forward(3)
    vx_end(-2)
    vx_end(2)
    k_step = kz_step(k_step, 4)
    vx_forward(4)
    vx_end(-3)
    vx_end(3)
    vx_end(4)
    kz_step(k_step, 5)
    for move in moves:
        move.wait()
    for copy in crossing:
        copy.wait_recv()
    for copy in sent:
        copy.wait_send()


def gather(queries, keys, values, d_out):
    whole = jax.ShapeDtypeStruct(WHOLE, jnp.bfloat16)
    part = jax.ShapeDtypeStruct((PIECES, HALF, GROUP * HD), jnp.bfloat16)
    dma = pltpu.SemaphoreType.DMA
    return pl.pallas_call(
        gather_kernel,
        out_shape=(whole, whole, part, part),
        in_specs=[ANY] * 4,
        out_specs=(ANY,) * 4,
        scratch_shapes=[
            dma((2, YN)), dma((2, YN)), dma((2, PIECES)), dma((2, PIECES)),
            dma((4,)), dma((4,)), dma((2, 5, 2)), dma((2, 5, 2)), dma((2, 5)), dma((2, 5)),
            dma((2, 2, ZN)), dma((2, 2, ZN)), dma((23,)), dma((23,)), dma((4,)),
        ],
        compiler_params=pltpu.CompilerParams(collective_id=0, has_side_effects=True),
        name="gather",
    )(queries, keys, values, d_out)


def attention_kernel(
    meta, touched, start_ref, q_ref, g_ref, ka_ref, va_ref, o_ref, dq_ref, dk_ref, dv_ref,
    kbuf, vbuf, sbuf, pbuf, dk_acc, dv_acc, flush, k_sem, v_sem, f_sem,
):
    scaling = HD ** (-0.5)
    factor = scaling * math.log2(math.e)

    def rows_of(j):
        return pl.ds(pl.multiple_of(j * KB, KB), KB)

    def fetches(i, slot, j):
        src = rows_of(meta[i, 0] + j)
        return (
            pltpu.make_async_copy(ka_ref.at[src], kbuf.at[slot, rows_of(j)], k_sem.at[slot, j]),
            pltpu.make_async_copy(va_ref.at[src], vbuf.at[slot, rows_of(j)], v_sem.at[slot, j]),
        )

    def fetch(i, slot):
        def body(j, carry):
            for copy in fetches(i, slot, j):
                copy.start()
            return carry

        lax.fori_loop(0, meta[i, 1], body, 0)

    def stacked(value):
        return jnp.concatenate([value[:, h * HD : (h + 1) * HD] for h in range(GROUP)], axis=0)

    def unstacked(value):
        return jnp.concatenate([value[h * HALF : (h + 1) * HALF] for h in range(GROUP)], axis=1)

    def mm(a, b, da, db):
        return lax.dot_general(
            a, b, (((da,), (db,)), ((), ())), preferred_element_type=jnp.float32
        )

    fetch(0, 0)

    def piece(i, seen):
        slot = lax.rem(i, 2)

        @pl.when(i + 1 < PIECES)
        def _():
            fetch(i + 1, 1 - slot)

        low, count, first = meta[i, 0], meta[i, 1], meta[i, 2]
        q = stacked(q_ref[i])
        g = stacked(g_ref[i])
        starts = start_ref[i]
        times = first + lax.rem(lax.broadcasted_iota(jnp.int32, (1, ROWS), 1), HALF)
        key_iota = lax.broadcasted_iota(jnp.int32, (KB, ROWS), 0)

        def scores_step(j, top):
            fetches(i, slot, j)[0].wait()
            s = mm(kbuf[slot, rows_of(j)], q, 1, 1)
            base = (low + j) * KB
            s = jnp.where((key_iota >= starts - base) & (key_iota <= times - base), s, NEG_FILL)
            sbuf[rows_of(j)] = s
            return jnp.maximum(top, jnp.max(s.reshape(KB // 8, 8, ROWS), axis=0))

        top = lax.fori_loop(0, count, scores_step, jnp.full((8, ROWS), NEG_FILL, jnp.float32))
        top = jnp.max(top, axis=0, keepdims=True)

        def weights_step(j, carry):
            total, out = carry
            fetches(i, slot, j)[1].wait()
            p = jnp.exp2((sbuf[rows_of(j)] - top) * factor)
            total = total + jnp.sum(p.reshape(KB // 8, 8, ROWS), axis=0)
            p = p.astype(jnp.bfloat16)
            pbuf[rows_of(j)] = p
            return total, out + mm(vbuf[slot, rows_of(j)], p, 0, 0)

        total, out = lax.fori_loop(
            0,
            count,
            weights_step,
            (jnp.zeros((8, ROWS), jnp.float32), jnp.zeros((HD, ROWS), jnp.float32)),
        )
        inverse = 1.0 / jnp.sum(total, axis=0, keepdims=True)
        out = (out * inverse).astype(jnp.bfloat16).astype(jnp.float32)
        o_ref[i] = unstacked(out.T.astype(jnp.bfloat16))
        g_turned = g.astype(jnp.float32).T
        delta = jnp.sum(g_turned * out, axis=0, keepdims=True) * inverse
        g_turned = g_turned * inverse
        g_rows = g_turned.T.astype(jnp.bfloat16)

        def clear(kb, carry):
            dk_acc[rows_of(kb)] = jnp.zeros((KB, HD), jnp.float32)
            dv_acc[rows_of(kb)] = jnp.zeros((KB, HD), jnp.float32)
            return carry

        lax.fori_loop(jnp.maximum(low, seen), low + count, clear, 0)

        def grad_step(j, dq):
            k = kbuf[slot, rows_of(j)]
            p = pbuf[rows_of(j)]
            gp = mm(vbuf[slot, rows_of(j)], g_rows, 1, 1)
            ds = (p.astype(jnp.float32) * (gp - delta)).astype(jnp.bfloat16)
            where = rows_of(low + j)
            dv_acc[where] += mm(p, g_rows, 1, 0)
            dk_acc[where] += mm(ds, q, 1, 0)
            return dq + mm(k, ds, 0, 0)

        dq = lax.fori_loop(0, count, grad_step, jnp.zeros((HD, ROWS), jnp.float32))
        dq_ref[i] = unstacked((dq * scaling).T.astype(jnp.bfloat16))
        return low + count

    lax.fori_loop(0, PIECES, piece, 0)

    def flushes(kb, slot):
        return (
            pltpu.make_async_copy(flush.at[0, slot], dk_ref.at[rows_of(kb)], f_sem.at[0, slot]),
            pltpu.make_async_copy(flush.at[1, slot], dv_ref.at[rows_of(kb)], f_sem.at[1, slot]),
        )

    def flush_step(kb, carry):
        slot = lax.rem(kb, 2)

        @pl.when(kb >= 2)
        def _():
            for copy in flushes(kb - 2, slot):
                copy.wait()

        @pl.when(touched[kb] > 0)
        def _():
            flush[0, slot] = (dk_acc[rows_of(kb)] * scaling).astype(jnp.bfloat16)
            flush[1, slot] = dv_acc[rows_of(kb)].astype(jnp.bfloat16)

        @pl.when(touched[kb] == 0)
        def _():
            flush[0, slot] = jnp.zeros((KB, HD), jnp.bfloat16)
            flush[1, slot] = jnp.zeros((KB, HD), jnp.bfloat16)

        for copy in flushes(kb, slot):
            copy.start()
        return carry

    lax.fori_loop(0, KBLOCKS, flush_step, 0)
    for kb in (KBLOCKS - 2, KBLOCKS - 1):
        for copy in flushes(kb, kb % 2):
            copy.wait()


def attention(lengths, q, g, keys, values):
    x, y, z, core = here()
    ends = jnp.cumsum(lengths)
    part = jnp.arange(PIECES, dtype=jnp.int32)
    block = (part // YN) * 128 + lax.rem(part, YN) * 32 + core * 16 + z * 2 + lax.rem(x, 2)
    first = block * 128 + (x // 2) * HALF
    times = first[:, None] + jnp.arange(HALF, dtype=jnp.int32)[None, :]
    starts = jnp.sum(
        jnp.where(ends[None, None, :] <= times[:, :, None], lengths[None, None, :], 0), axis=2
    )
    low = starts[:, 0] // KB
    high = (first + HALF - 1) // KB
    meta = jnp.stack([low, high - low + 1, first], axis=1).astype(jnp.int32)
    block_ids = jnp.arange(KBLOCKS, dtype=jnp.int32)[:, None]
    touched = jnp.any((block_ids >= low[None]) & (block_ids <= high[None]), axis=1)
    start_rows = jnp.tile(starts, (1, GROUP)).reshape(PIECES, 1, ROWS).astype(jnp.int32)
    part_shape = jax.ShapeDtypeStruct((PIECES, HALF, GROUP * HD), jnp.bfloat16)
    whole = jax.ShapeDtypeStruct((SEQ, HD), jnp.bfloat16)
    dma = pltpu.SemaphoreType.DMA
    return pl.pallas_call(
        attention_kernel,
        out_shape=(part_shape, part_shape, whole, whole),
        in_specs=[SMEM, SMEM, VMEM, VMEM, VMEM, ANY, ANY],
        out_specs=(VMEM, VMEM, ANY, ANY),
        scratch_shapes=[
            pltpu.VMEM((2, SPAN * KB, HD), jnp.bfloat16),
            pltpu.VMEM((2, SPAN * KB, HD), jnp.bfloat16),
            pltpu.VMEM((SPAN * KB, ROWS), jnp.float32),
            pltpu.VMEM((SPAN * KB, ROWS), jnp.bfloat16),
            pltpu.VMEM((SEQ, HD), jnp.float32),
            pltpu.VMEM((SEQ, HD), jnp.float32),
            pltpu.VMEM((2, 2, KB, HD), jnp.bfloat16),
            dma((2, SPAN)),
            dma((2, SPAN)),
            dma((2, 2)),
        ],
        compiler_params=pltpu.CompilerParams(vmem_limit_bytes=62 << 20),
        name="attention",
    )(
        meta,
        touched.astype(jnp.int32),
        start_rows,
        q,
        g,
        keys.reshape(SEQ, HD),
        values.reshape(SEQ, HD),
    )


def scatter_kernel(
    o_ref, dq_ref, dk_ref, dv_ref, ao_ref, gq_ref, gk_ref, gv_ref,
    own, part, kz_in, kx_half, kx_in, vx_half, vx_in, vz_in,
    own_sem, c_send, c_recv, kz_send, kz_recv, kx_send, kx_recv, vx_send, vx_recv,
    vz_send, vz_recv, p_send, p_recv, y_send, y_recv, local,
):
    at = Spot()
    greet(at.peers())
    ours = [dk_ref, dv_ref]
    sent, moves = [], []

    def go(src, dst, send, recv, peer):
        copy = remote(src, dst, send, recv, peer)
        copy.start()
        sent.append(copy)
        return copy

    waiting = {}
    for dz in (4, 3, -3, 2, -2, 1, -1, 0):
        for number in range(2):
            place = (number, dz + 3)
            load = pltpu.make_async_copy(
                at.across_x(ours[number], at.core, dz), own.at[place], own_sem.at[place]
            )
            load.start()
            theirs = go(
                at.across_x(ours[number], 1 - at.core, dz),
                part.at[place],
                c_send.at[place],
                c_recv.at[place],
                at.partner,
            )
            waiting[number, dz] = (load, theirs)

    def f32(value):
        return value.astype(jnp.float32)

    def joined(number, dz):
        load, theirs = waiting[number, dz]
        load.wait()
        theirs.wait_recv()
        place = (number, dz + 3)
        for xh in range(XHI):
            total = f32(own[(*place, xh)]) + f32(part[(*place, xh)])
            own[(*place, xh)] = total.astype(jnp.bfloat16)

    def add(place, value):
        own[place] = (f32(own[place]) + f32(value)).astype(jnp.bfloat16)

    def kz(step, half, way):
        dz = (5 - step) if way == 0 else (step - 5)
        dz = 4 if dz == -4 else dz
        place = (way, step - 1, half)
        return go(
            own.at[0, dz + 3, :, halves(half)],
            kz_in.at[place],
            kz_send.at[place],
            kz_recv.at[place],
            at.z_peer[way],
        )

    def kz_step(before, step):
        after = {}
        for way in range(2):
            dz = (5 - step) if way == 0 else (step - 5)
            joined(0, dz)
            for half in range(2):
                if (half, way) in before:
                    before[half, way].wait_recv()
                    add((0, dz + 3, slice(None), halves(half)), kz_in[way, step - 2, half])
                after[half, way] = kz(step, half, way)
        return after

    def edge(dx):
        x = at.x_at(dx)
        return x // 2, lax.rem(x, 2)

    def own_chunk(number, dz, dx, half=None):
        xh, xl = edge(dx)
        return (number, dz + 3, xh, halves(half), xl)

    def x_first(number, dz, inbox, send, recv):
        out = []
        for way in range(2):
            place = (dz + 3, way) if number else (way,)
            sem = (0, *place)
            out.append(
                go(
                    own.at[own_chunk(number, dz, 2, way)],
                    inbox.at[place],
                    send.at[sem],
                    recv.at[sem],
                    at.x_peer[way],
                )
            )
        return out

    def x_second(number, dz, first, half_box, inbox, send, recv):
        out = []
        for way in range(2):
            place = (dz + 3, way) if number else (way,)
            sem = (1, *place)
            dx = 1 - 2 * way
            first[way].wait_recv()
            add(own_chunk(number, dz, dx, way), half_box[place])
            out.append(
                go(
                    own.at[own_chunk(number, dz, dx)],
                    inbox.at[place],
                    send.at[sem],
                    recv.at[sem],
                    at.x_peer[way],
                )
            )
        return out

    def x_third(number, dz, second, inbox):
        for way in range(2):
            place = (dz + 3, way) if number else (way,)
            second[way].wait_recv()
        places = [(dz + 3, way) if number else (way,) for way in range(2)]
        mine = own_chunk(number, dz, 0)
        total = f32(own[mine]) + f32(inbox[places[0]]) + f32(inbox[places[1]])
        own[mine] = total.astype(jnp.bfloat16)

    v_first, v_second = {}, {}

    def va(dz):
        joined(1, dz)
        v_first[dz] = x_first(1, dz, vx_half, vx_send, vx_recv)

    def vb(dz):
        v_second[dz] = x_second(1, dz, v_first[dz], vx_half, vx_in, vx_send, vx_recv)

    def vc(dz):
        x_third(1, dz, v_second[dz], vx_in)

    v_step = [None, None]

    def vz(step):
        for way in range(2):
            dz = (5 - step) if way == 0 else (step - 5)
            dz = 4 if dz == -4 else dz
            half = way if step == 1 else None
            if step == 2:
                v_step[way].wait_recv()
                add(own_chunk(1, dz, 0, way), vz_in[way, 0, halves(way)])
            elif step > 2:
                v_step[way].wait_recv()
                add(own_chunk(1, dz, 0), vz_in[way, step - 2])
            place = (way, step - 1)
            v_step[way] = go(
                own.at[own_chunk(1, dz, 0, half)],
                vz_in.at[(*place, halves(half))],
                vz_send.at[place],
                vz_recv.at[place],
                at.z_peer[way],
            )

    joined(0, 4)
    k_step = {(way, way): kz(1, way, way) for way in range(2)}
    va(4)
    va(3)
    va(-3)
    for number, (src, dst) in enumerate([(o_ref, ao_ref), (dq_ref, gq_ref)]):
        for place, (dx, dy) in enumerate(at.offsets):
            xh, y = at.part_of(dx, dy)
            piece = src.at[xh * YN + y]
            slot = dst.at[
                pl.ds(pl.multiple_of(at.xh * HALF, HALF), HALF), lanes(at.y, GROUP * HD)
            ]
            if place == 0:
                move = pltpu.make_async_copy(piece, slot, local.at[number])
            else:
                move = remote(
                    piece,
                    slot,
                    p_send.at[number, place],
                    p_recv.at[number, place],
                    at.part_device(dx, dy),
                )
            move.start()
            moves.append(move)
    vb(4)
    va(2)
    va(-2)
    k_step = kz_step(k_step, 2)
    vb(3)
    vb(-3)
    vc(4)
    vz(1)
    va(1)
    va(-1)
    vb(2)
    vb(-2)
    vc(3)
    vc(-3)
    vz(2)
    va(0)
    k_step = kz_step(k_step, 3)
    vb(1)
    vb(-1)
    vc(2)
    vc(-2)
    vz(3)
    vb(0)
    vc(1)
    vc(-1)
    vz(4)
    k_step = kz_step(k_step, 4)
    vc(0)

    def finish(number, ref):
        for dy in range(YN):
            _, y = at.part_of(0, dy)
            xh, xl = edge(0)
            piece = own.at[number, 3, xh, y, xl]
            slot = ref.at[:, lanes(at.y, HD)]
            if dy == 0:
                move = pltpu.make_async_copy(piece, slot, local.at[2 + number])
            else:
                move = remote(
                    piece,
                    slot,
                    y_send.at[number, dy],
                    y_recv.at[number, dy],
                    at.part_device(0, dy),
                )
            move.start()
            moves.append(move)

    joined(0, 0)
    for half in range(2):
        for way in range(2):
            k_step[half, way].wait_recv()
        where = (0, 3, slice(None), halves(half))
        total = f32(own[where]) + f32(kz_in[0, 3, half]) + f32(kz_in[1, 3, half])
        own[where] = total.astype(jnp.bfloat16)
    first = x_first(0, 0, kx_half, kx_send, kx_recv)
    for way in range(2):
        v_step[way].wait_recv()
    mine = own_chunk(1, 0, 0)
    total = f32(own[mine]) + f32(vz_in[0, 3]) + f32(vz_in[1, 3])
    own[mine] = total.astype(jnp.bfloat16)
    finish(1, gv_ref)
    second = x_second(0, 0, first, kx_half, kx_in, kx_send, kx_recv)
    x_third(0, 0, second, kx_in)
    finish(0, gk_ref)
    for move in moves:
        move.wait()
    for copy in sent:
        copy.wait_send()


def scatter(out, dq, dk, dv):
    tokens = jax.ShapeDtypeStruct((128, QH * HD), jnp.bfloat16)
    pairs = jax.ShapeDtypeStruct((128, KVH * HD), jnp.bfloat16)
    dma = pltpu.SemaphoreType.DMA

    def box(*shape):
        return pltpu.VMEM((*shape, 128, HD), jnp.bfloat16)

    return pl.pallas_call(
        scatter_kernel,
        out_shape=(tokens, tokens, pairs, pairs),
        in_specs=[ANY] * 4,
        out_specs=(ANY,) * 4,
        scratch_shapes=[
            box(2, ZN, XHI, YN, XLO),
            box(2, ZN, XHI, YN, XLO),
            box(2, 4, 2, XHI, 2, XLO),
            box(2, 2),
            box(2, YN),
            box(ZN, 2, 2),
            box(ZN, 2, YN),
            box(2, 4, YN),
            dma((2, ZN)), dma((2, ZN)), dma((2, ZN)), dma((2, 4, 2)), dma((2, 4, 2)),
            dma((2, 2)), dma((2, 2)), dma((2, ZN, 2)), dma((2, ZN, 2)), dma((2, 4)), dma((2, 4)),
            dma((2, PIECES)), dma((2, PIECES)), dma((2, YN)), dma((2, YN)), dma((4,)),
        ],
        compiler_params=pltpu.CompilerParams(
            collective_id=1, has_side_effects=True, vmem_limit_bytes=48 << 20
        ),
        name="scatter",
    )(out, dq, dk.reshape(WHOLE), dv.reshape(WHOLE))


def shards(queries, keys, values, d_out, lengths):
    ka, va, q, g = gather(queries, keys, values, d_out)
    out, dq, dk, dv = attention(lengths, q, g, ka, va)
    return scatter(out, dq, dk, dv)


def solution(mesh):
    spec = P(("ctx", "head"), None)
    return jax.shard_map(
        shards,
        mesh=mesh,
        in_specs=(spec, spec, spec, spec, P()),
        out_specs=(spec,) * 4,
        check_vma=False,
    )
```

```python
import functools
import math

import jax
import jax.numpy as jnp
from jax import lax
from jax.experimental import pallas as pl
from jax.experimental.pallas import tpu as pltpu
from jax.sharding import PartitionSpec as P

QH = 16
KVH = 4
HD = 128
GROUP = QH // KVH
SEQ = 32768
DOC_MOST = 8192
NEG_FILL = -1e30

XHI, XN, YN, ZN, XLO = 2, 4, 4, 8, 2
WHOLE = (XHI, YN, 2, ZN, XLO, 128, 128)
HALF = 64
PIECES = XHI * YN
ROWS = GROUP * HALF
KB = 512
UNITS = 4
KBLOCKS = SEQ // KB
SPAN = (DOC_MOST + HALF - 1 + KB - 1) // KB
FLUSH_SLOTS = 4

MESH = pl.DeviceIdType.MESH
ANY = pl.BlockSpec(memory_space=pl.ANY)
VMEM = pl.BlockSpec(memory_space=pltpu.VMEM)
SMEM = pl.BlockSpec(memory_space=pltpu.SMEM)


def here():
    c = lax.axis_index("ctx")
    h = lax.axis_index("head")
    xh, y, core = c // 8, lax.rem(c // 2, 4), lax.rem(c, 2)
    z, xl = h // 2, lax.rem(h, 2)
    return xh * 2 + xl, y, z, core


def device(x, y, z, core):
    return ((x // 2) * 8 + y * 2 + core, z * 2 + lax.rem(x, 2))


def greet(peers):
    barrier = pltpu.get_barrier_semaphore()
    for peer in peers:
        pl.semaphore_signal(barrier, inc=1, device_id=peer, device_id_type=MESH)
    pl.semaphore_wait(barrier, len(peers))


def remote(src, dst, send, recv, peer):
    return pltpu.make_async_remote_copy(
        src_ref=src, dst_ref=dst, send_sem=send, recv_sem=recv, device_id=peer, device_id_type=MESH
    )


def lanes(start, size):
    return pl.ds(pl.multiple_of(start * size, size), size)


class Spot:
    def __init__(self):
        self.x, self.y, self.z, self.core = here()
        self.xh, self.xl = self.x // 2, lax.rem(self.x, 2)
        self.x_peer = [device(self.x_at(d), self.y, self.z, self.core) for d in (1, -1)]
        self.z_peer = [device(self.x, self.y, self.z_at(d), self.core) for d in (1, -1)]
        self.partner = device(self.x, self.y, self.z, 1 - self.core)
        self.offsets = [(dx, dy) for dx in range(XHI) for dy in range(YN)]

    def x_at(self, d):
        return lax.rem(self.x + d + XN, XN)

    def z_at(self, d):
        return lax.rem(self.z + d + ZN, ZN)

    def part_of(self, dx, dy):
        return lax.rem(self.xh + dx, XHI), lax.rem(self.y + dy, YN)

    def part_device(self, dx, dy):
        xh, y = self.part_of(dx, dy)
        return device(xh * 2 + self.xl, y, self.z, self.core)

    def peers(self):
        return (
            self.x_peer
            + self.z_peer
            + [self.partner]
            + [self.part_device(dx, dy) for dx, dy in self.offsets[1:]]
        )

    def across_x(self, ref, core, dz, half=None):
        return ref.at[:, halves(half), core, self.z_at(dz)]

    def chunk(self, ref, dx, dz, half=None):
        x = self.x_at(dx)
        return ref.at[x // 2, halves(half), self.core, self.z_at(dz), lax.rem(x, 2)]


def halves(half):
    return pl.ds(0, YN) if half is None else pl.ds(half * 2, 2)


def gather_kernel(
    q_ref, k_ref, v_ref, g_ref, ka_ref, va_ref, qi_ref, gi_ref,
    y_send, y_recv, p_send, p_recv, kx_send, kx_recv, kz_send, kz_recv, vz_send, vz_recv,
    vx_send, vx_recv, c_send, c_recv, local,
):
    at = Spot()
    greet(at.peers())
    copies = []
    for number, (src, dst) in enumerate([(k_ref, ka_ref), (v_ref, va_ref)]):
        slot = dst.at[at.xh, at.y, at.core, at.z, at.xl]
        keep = pltpu.make_async_copy(src.at[:, lanes(at.y, HD)], slot, local.at[number])
        keep.start()
        copies.append([keep])
        for dy in range(1, YN):
            _, y = at.part_of(0, dy)
            send = remote(
                src.at[:, lanes(y, HD)],
                slot,
                y_send.at[number, dy],
                y_recv.at[number, dy],
                at.part_device(0, dy),
            )
            send.start()
            copies[number].append(send)

    sent, crossing = [], []

    def go(piece, send, recv, peer):
        copy = remote(piece, piece, send, recv, peer)
        copy.start()
        sent.append(copy)
        return copy

    def cross(piece):
        number = len(crossing)
        crossing.append(go(piece, c_send.at[number], c_recv.at[number], at.partner))

    def kx(number, piece, way):
        return go(piece, kx_send.at[number], kx_recv.at[number], at.x_peer[way])

    def kz(step, half, way):
        dz = (1 - step) if way == 0 else (step - 1)
        piece = at.across_x(ka_ref, at.core, dz, half)
        place = (way, step, half)
        return go(piece, kz_send.at[place], kz_recv.at[place], at.z_peer[way])

    def vz(step, way):
        dz = (1 - step) if way == 0 else (step - 1)
        piece = at.chunk(va_ref, 0, dz, way if step == 4 else None)
        return go(piece, vz_send.at[way, step], vz_recv.at[way, step], at.z_peer[way])

    vx_first, vx_second = {}, {}

    def vx(stage, way, dz, piece):
        place = (stage, way, dz + 3)
        return go(piece, vx_send.at[place], vx_recv.at[place], at.x_peer[way])

    def vx_start(dz):
        vx_first[dz] = [vx(0, way, dz, at.chunk(va_ref, 0, dz)) for way in range(2)]

    def vx_forward(dz):
        vx_second[dz] = []
        for way in range(2):
            vx_first[dz][way].wait_recv()
            piece = at.chunk(va_ref, 2 * way - 1, dz, way)
            vx_second[dz].append(vx(1, way, dz, piece))

    def vx_end(dz):
        for copy in vx_second[dz]:
            copy.wait_recv()
        cross(at.across_x(va_ref, at.core, dz))

    def kz_step(before, step):
        after = {}
        for half in range(2):
            for way in range(2):
                if (half, way) not in before:
                    continue
                before[half, way].wait_recv()
                if step < 4 or (step == 4 and half == way):
                    after[half, way] = kz(step, half, way)
                dz = (1 - step) if way == 0 else (step - 1)
                cross(at.across_x(ka_ref, at.core, dz, half))
        return after

    for copy in copies[0]:
        copy.wait()
    k_first = [kx(way, at.chunk(ka_ref, 0, 0), way) for way in range(2)]
    for copy in copies[1]:
        copy.wait()
    v_step = [vz(1, way) for way in range(2)]
    k_second = []
    for way in range(2):
        k_first[way].wait_recv()
        k_second.append(kx(2 + way, at.chunk(ka_ref, 2 * way - 1, 0, way), way))
    vx_start(0)

    def vz_next(step):
        for way in range(2):
            v_step[way].wait_recv()
            v_step[way] = vz(step, way)
            vx_start((1 - step) if way == 0 else (step - 1))

    vz_next(2)
    for copy in k_second:
        copy.wait_recv()
    k_step = {(half, way): kz(1, half, way) for half in range(2) for way in range(2)}
    cross(at.across_x(ka_ref, at.core, 0))
    vz_next(3)
    vx_forward(0)
    vz_next(4)
    vx_forward(-1)
    vx_forward(1)
    vx_end(0)
    for way in range(2):
        v_step[way].wait_recv()
    vx_start(4)
    k_step = kz_step(k_step, 2)
    vx_forward(-2)
    vx_forward(2)
    vx_end(-1)
    vx_end(1)
    k_step = kz_step(k_step, 3)
    moves = []
    for number, (src, dst) in enumerate([(q_ref, qi_ref), (g_ref, gi_ref)]):
        for place, (dx, dy) in enumerate(at.offsets):
            xh, y = at.part_of(dx, dy)
            piece = src.at[pl.ds(pl.multiple_of(xh * HALF, HALF), HALF), lanes(y, GROUP * HD)]
            slot = dst.at[at.xh * YN + at.y]
            if place == 0:
                move = pltpu.make_async_copy(piece, slot, local.at[2 + number])
            else:
                move = remote(
                    piece,
                    slot,
                    p_send.at[number, place],
                    p_recv.at[number, place],
                    at.part_device(dx, dy),
                )
            move.start()
            moves.append(move)

    vx_forward(-3)
    vx_forward(3)
    vx_end(-2)
    vx_end(2)
    k_step = kz_step(k_step, 4)
    vx_forward(4)
    vx_end(-3)
    vx_end(3)
    vx_end(4)
    kz_step(k_step, 5)
    for move in moves:
        move.wait()
    for copy in crossing:
        copy.wait_recv()
    for copy in sent:
        copy.wait_send()


def gather(queries, keys, values, d_out):
    whole = jax.ShapeDtypeStruct(WHOLE, jnp.bfloat16)
    part = jax.ShapeDtypeStruct((PIECES, HALF, GROUP * HD), jnp.bfloat16)
    dma = pltpu.SemaphoreType.DMA
    return pl.pallas_call(
        gather_kernel,
        out_shape=(whole, whole, part, part),
        in_specs=[ANY] * 4,
        out_specs=(ANY,) * 4,
        scratch_shapes=[
            dma((2, YN)), dma((2, YN)), dma((2, PIECES)), dma((2, PIECES)),
            dma((4,)), dma((4,)), dma((2, 5, 2)), dma((2, 5, 2)), dma((2, 5)), dma((2, 5)),
            dma((2, 2, ZN)), dma((2, 2, ZN)), dma((23,)), dma((23,)), dma((4,)),
        ],
        compiler_params=pltpu.CompilerParams(collective_id=0, has_side_effects=True),
        name="gather",
    )(queries, keys, values, d_out)


def attention_kernel(
    meta, first_use, last_use, start_ref, q_ref, g_ref, ka_ref, va_ref, o_ref, dq_ref, dk_ref,
    dv_ref, kbuf, vbuf, sbuf, pbuf, dk_acc, dv_acc, flush, zeros, pending, k_sem, v_sem, f_sem,
    z_sem,
):
    scaling = HD ** (-0.5)
    factor = scaling * math.log2(math.e)

    def block(j, size=KB):
        return pl.ds(pl.multiple_of(j * KB, KB), size)

    def span(low, j, size=KB):
        return pl.ds(pl.multiple_of(low + j * KB, HALF), size)

    def fetches(i, slot, j):
        src = span(meta[i, 0], j)
        return (
            pltpu.make_async_copy(ka_ref.at[src], kbuf.at[slot, block(j)], k_sem.at[slot, j]),
            pltpu.make_async_copy(va_ref.at[src], vbuf.at[slot, block(j)], v_sem.at[slot, j]),
        )

    def fetch(i, slot):
        def body(j, carry):
            for copy in fetches(i, slot, j):
                copy.start()
            return carry

        lax.fori_loop(0, meta[i, 1], body, 0)

    def stacked(value):
        return jnp.concatenate([value[:, h * HD : (h + 1) * HD] for h in range(GROUP)], axis=0)

    def unstacked(value):
        return jnp.concatenate([value[h * HALF : (h + 1) * HALF] for h in range(GROUP)], axis=1)

    def mm(a, b, da, db):
        return lax.dot_general(
            a, b, (((da,), (db,)), ((), ())), preferred_element_type=jnp.float32
        )

    def in_pairs(count, body, carry):
        carry = lax.fori_loop(
            0, count // UNITS, lambda j, c: body(UNITS * j, UNITS * KB, c), carry
        )
        done, units = count // UNITS * UNITS, UNITS // 2
        while units:
            more = lax.rem(count // units, 2)
            carry = lax.cond(
                more == 1,
                lambda c, done=done, units=units: body(done, units * KB, c),
                lambda c: c,
                carry,
            )
            done, units = done + more * units, units // 2
        return carry

    def blanks(kb):
        return (
            pltpu.make_async_copy(zeros, dk_ref.at[block(kb)], z_sem.at[0, kb]),
            pltpu.make_async_copy(zeros, dv_ref.at[block(kb)], z_sem.at[1, kb]),
        )

    def flushes(kb, slot):
        return (
            pltpu.make_async_copy(flush.at[0, slot], dk_ref.at[block(kb)], f_sem.at[0, slot]),
            pltpu.make_async_copy(flush.at[1, slot], dv_ref.at[block(kb)], f_sem.at[1, slot]),
        )

    fetch(0, 0)
    zeros[...] = jnp.zeros((KB, HD), jnp.bfloat16)
    for slot in range(FLUSH_SLOTS):
        pending[slot] = 0

    def blank_start(kb, carry):
        @pl.when(first_use[kb] < 0)
        def _():
            for copy in blanks(kb):
                copy.start()

        return carry

    lax.fori_loop(0, KBLOCKS, blank_start, 0)

    def piece(i, carry):
        slot = lax.rem(i, 2)

        @pl.when(i + 1 < PIECES)
        def _():
            fetch(i + 1, 1 - slot)

        low, count, first, last_start = meta[i, 0], meta[i, 1], meta[i, 2], meta[i, 3]
        q = stacked(q_ref[i])
        g = stacked(g_ref[i])
        starts = start_ref[i]
        times = first + lax.rem(lax.broadcasted_iota(jnp.int32, (1, ROWS), 1), HALF)

        def scores_step(j, size, top):
            for part in range(size // KB):
                fetches(i, slot, j + part)[0].wait()
            base = low + j * KB

            def finish(s):
                sbuf[block(j, size)] = s
                return jnp.maximum(top, jnp.max(s.reshape(size // 8, 8, ROWS), axis=0))

            def scores():
                return mm(kbuf[slot, block(j, size)], q, 1, 1)

            def masked():
                key = lax.broadcasted_iota(jnp.int32, (size, ROWS), 0)
                seen = (key >= starts - base) & (key <= times - base)
                return finish(jnp.where(seen, scores(), NEG_FILL))

            whole = (base >= last_start) & (base + size - 1 <= first)
            return lax.cond(whole, lambda: finish(scores()), masked)

        top = in_pairs(count, scores_step, jnp.full((8, ROWS), NEG_FILL, jnp.float32))
        top = jnp.max(top, axis=0, keepdims=True)

        def weights_step(j, size, carry):
            total, out = carry
            for part in range(size // KB):
                fetches(i, slot, j + part)[1].wait()
            p = jnp.exp2((sbuf[block(j, size)] - top) * factor)
            total = total + jnp.sum(p.reshape(size // 8, 8, ROWS), axis=0)
            p = p.astype(jnp.bfloat16)
            pbuf[block(j, size)] = p
            return total, out + mm(vbuf[slot, block(j, size)], p, 0, 0)

        total, out = in_pairs(
            count,
            weights_step,
            (jnp.zeros((8, ROWS), jnp.float32), jnp.zeros((HD, ROWS), jnp.float32)),
        )
        inverse = 1.0 / jnp.sum(total, axis=0, keepdims=True)
        out = (out * inverse).astype(jnp.bfloat16).astype(jnp.float32)
        o_ref[i] = unstacked(out.T.astype(jnp.bfloat16))
        g_turned = g.astype(jnp.float32).T
        delta = jnp.sum(g_turned * out, axis=0, keepdims=True) * inverse
        g_rows = (g_turned * inverse).T.astype(jnp.bfloat16)
        block_low, block_end = low // KB, (low + count * KB - 1) // KB + 1

        def clear(kb, carry):
            @pl.when(first_use[kb] == i)
            def _():
                dk_acc[block(kb)] = jnp.zeros((KB, HD), jnp.float32)
                dv_acc[block(kb)] = jnp.zeros((KB, HD), jnp.float32)

            return carry

        lax.fori_loop(block_low, block_end, clear, 0)

        def grad_step(j, size, dq):
            k = kbuf[slot, block(j, size)]
            p = pbuf[block(j, size)]
            gp = mm(vbuf[slot, block(j, size)], g_rows, 1, 1)
            ds = (p.astype(jnp.float32) * (gp - delta)).astype(jnp.bfloat16)
            where = span(low, j, size)
            dv_acc[where] += mm(p, g_rows, 1, 0)
            dk_acc[where] += mm(ds, q, 1, 0)
            return dq + mm(k, ds, 0, 0)

        dq = in_pairs(count, grad_step, jnp.zeros((HD, ROWS), jnp.float32))
        dq_ref[i] = unstacked((dq * scaling).T.astype(jnp.bfloat16))

        def flush_step(kb, carry):
            @pl.when(last_use[kb] == i)
            def _():
                slot = lax.rem(kb, FLUSH_SLOTS)

                @pl.when(pending[slot] > 0)
                def _():
                    for copy in flushes(kb, slot):
                        copy.wait()

                pending[slot] = 1
                flush[0, slot] = (dk_acc[block(kb)] * scaling).astype(jnp.bfloat16)
                flush[1, slot] = dv_acc[block(kb)].astype(jnp.bfloat16)
                for copy in flushes(kb, slot):
                    copy.start()

            return carry

        lax.fori_loop(block_low, block_end, flush_step, 0)
        return carry

    lax.fori_loop(0, PIECES, piece, 0)
    for slot in range(FLUSH_SLOTS):

        @pl.when(pending[slot] > 0)
        def _():
            for copy in flushes(0, slot):
                copy.wait()

    def blank_wait(kb, carry):
        @pl.when(first_use[kb] < 0)
        def _():
            for copy in blanks(kb):
                copy.wait()

        return carry

    lax.fori_loop(0, KBLOCKS, blank_wait, 0)


def attention(lengths, q, g, keys, values):
    x, y, z, core = here()
    ends = jnp.cumsum(lengths)
    part = jnp.arange(PIECES, dtype=jnp.int32)
    tile = (part // YN) * 128 + lax.rem(part, YN) * 32 + core * 16 + z * 2 + lax.rem(x, 2)
    first = tile * 128 + (x // 2) * HALF
    times = first[:, None] + jnp.arange(HALF, dtype=jnp.int32)[None, :]
    starts = jnp.sum(
        jnp.where(ends[None, None, :] <= times[:, :, None], lengths[None, None, :], 0), axis=2
    )
    end = first + HALF
    count = (end - starts[:, 0] + KB - 1) // KB
    low = jnp.maximum(end - count * KB, 0)
    meta = jnp.stack([low, count, first, starts[:, HALF - 1]], axis=1).astype(jnp.int32)
    ids = jnp.arange(KBLOCKS, dtype=jnp.int32)[:, None]
    used = (ids >= low[None] // KB) & (ids <= (low + count * KB - 1)[None] // KB)
    last_use = jnp.max(jnp.where(used, part[None], -1), axis=1)
    first_use = jnp.min(jnp.where(used, part[None], PIECES), axis=1)
    first_use = jnp.where(last_use < 0, -1, first_use)
    start_rows = jnp.tile(starts, (1, GROUP)).reshape(PIECES, 1, ROWS).astype(jnp.int32)
    part_shape = jax.ShapeDtypeStruct((PIECES, HALF, GROUP * HD), jnp.bfloat16)
    whole = jax.ShapeDtypeStruct((SEQ, HD), jnp.bfloat16)
    dma = pltpu.SemaphoreType.DMA
    return pl.pallas_call(
        attention_kernel,
        out_shape=(part_shape, part_shape, whole, whole),
        in_specs=[SMEM, SMEM, SMEM, VMEM, VMEM, VMEM, ANY, ANY],
        out_specs=(VMEM, VMEM, ANY, ANY),
        scratch_shapes=[
            pltpu.VMEM((2, SPAN * KB, HD), jnp.bfloat16),
            pltpu.VMEM((2, SPAN * KB, HD), jnp.bfloat16),
            pltpu.VMEM((SPAN * KB, ROWS), jnp.float32),
            pltpu.VMEM((SPAN * KB, ROWS), jnp.bfloat16),
            pltpu.VMEM((SEQ, HD), jnp.float32),
            pltpu.VMEM((SEQ, HD), jnp.float32),
            pltpu.VMEM((2, FLUSH_SLOTS, KB, HD), jnp.bfloat16),
            pltpu.VMEM((KB, HD), jnp.bfloat16),
            pltpu.SMEM((FLUSH_SLOTS,), jnp.int32),
            dma((2, SPAN)),
            dma((2, SPAN)),
            dma((2, FLUSH_SLOTS)),
            dma((2, KBLOCKS)),
        ],
        compiler_params=pltpu.CompilerParams(vmem_limit_bytes=62 << 20),
        name="attention",
    )(
        meta,
        first_use.astype(jnp.int32),
        last_use.astype(jnp.int32),
        start_rows,
        q,
        g,
        keys.reshape(SEQ, HD),
        values.reshape(SEQ, HD),
    )


def scatter_kernel(
    o_ref, dq_ref, dk_ref, dv_ref, ao_ref, gq_ref, gk_ref, gv_ref,
    own, part, kz_in, kx_half, kx_in, vx_half, vx_in, vz_in,
    own_sem, c_send, c_recv, kz_send, kz_recv, kx_send, kx_recv, vx_send, vx_recv,
    vz_send, vz_recv, p_send, p_recv, y_send, y_recv, local,
):
    at = Spot()
    greet(at.peers())
    ours = [dk_ref, dv_ref]
    sent, moves = [], []

    def go(src, dst, send, recv, peer):
        copy = remote(src, dst, send, recv, peer)
        copy.start()
        sent.append(copy)
        return copy

    waiting = {}
    for dz in (4, 3, -3, 2, -2, 1, -1, 0):
        for number in range(2):
            place = (number, dz + 3)
            load = pltpu.make_async_copy(
                at.across_x(ours[number], at.core, dz), own.at[place], own_sem.at[place]
            )
            load.start()
            theirs = go(
                at.across_x(ours[number], 1 - at.core, dz),
                part.at[place],
                c_send.at[place],
                c_recv.at[place],
                at.partner,
            )
            waiting[number, dz] = (load, theirs)

    def f32(value):
        return value.astype(jnp.float32)

    def joined(number, dz):
        load, theirs = waiting[number, dz]
        load.wait()
        theirs.wait_recv()
        place = (number, dz + 3)
        for xh in range(XHI):
            total = f32(own[(*place, xh)]) + f32(part[(*place, xh)])
            own[(*place, xh)] = total.astype(jnp.bfloat16)

    def add(place, value):
        own[place] = (f32(own[place]) + f32(value)).astype(jnp.bfloat16)

    def kz(step, half, way):
        dz = (5 - step) if way == 0 else (step - 5)
        dz = 4 if dz == -4 else dz
        place = (way, step - 1, half)
        return go(
            own.at[0, dz + 3, :, halves(half)],
            kz_in.at[place],
            kz_send.at[place],
            kz_recv.at[place],
            at.z_peer[way],
        )

    def kz_step(before, step):
        after = {}
        for way in range(2):
            dz = (5 - step) if way == 0 else (step - 5)
            joined(0, dz)
            for half in range(2):
                if (half, way) in before:
                    before[half, way].wait_recv()
                    add((0, dz + 3, slice(None), halves(half)), kz_in[way, step - 2, half])
                after[half, way] = kz(step, half, way)
        return after

    def edge(dx):
        x = at.x_at(dx)
        return x // 2, lax.rem(x, 2)

    def own_chunk(number, dz, dx, half=None):
        xh, xl = edge(dx)
        return (number, dz + 3, xh, halves(half), xl)

    def x_first(number, dz, inbox, send, recv):
        out = []
        for way in range(2):
            place = (dz + 3, way) if number else (way,)
            sem = (0, *place)
            out.append(
                go(
                    own.at[own_chunk(number, dz, 2, way)],
                    inbox.at[place],
                    send.at[sem],
                    recv.at[sem],
                    at.x_peer[way],
                )
            )
        return out

    def x_second(number, dz, first, half_box, inbox, send, recv):
        out = []
        for way in range(2):
            place = (dz + 3, way) if number else (way,)
            sem = (1, *place)
            dx = 1 - 2 * way
            first[way].wait_recv()
            add(own_chunk(number, dz, dx, way), half_box[place])
            out.append(
                go(
                    own.at[own_chunk(number, dz, dx)],
                    inbox.at[place],
                    send.at[sem],
                    recv.at[sem],
                    at.x_peer[way],
                )
            )
        return out

    def x_third(number, dz, second, inbox):
        for way in range(2):
            place = (dz + 3, way) if number else (way,)
            second[way].wait_recv()
        places = [(dz + 3, way) if number else (way,) for way in range(2)]
        mine = own_chunk(number, dz, 0)
        total = f32(own[mine]) + f32(inbox[places[0]]) + f32(inbox[places[1]])
        own[mine] = total.astype(jnp.bfloat16)

    v_first, v_second = {}, {}

    def va(dz):
        joined(1, dz)
        v_first[dz] = x_first(1, dz, vx_half, vx_send, vx_recv)

    def vb(dz):
        v_second[dz] = x_second(1, dz, v_first[dz], vx_half, vx_in, vx_send, vx_recv)

    def vc(dz):
        x_third(1, dz, v_second[dz], vx_in)

    v_step = [None, None]

    def vz(step):
        for way in range(2):
            dz = (5 - step) if way == 0 else (step - 5)
            dz = 4 if dz == -4 else dz
            half = way if step == 1 else None
            if step == 2:
                v_step[way].wait_recv()
                add(own_chunk(1, dz, 0, way), vz_in[way, 0, halves(way)])
            elif step > 2:
                v_step[way].wait_recv()
                add(own_chunk(1, dz, 0), vz_in[way, step - 2])
            place = (way, step - 1)
            v_step[way] = go(
                own.at[own_chunk(1, dz, 0, half)],
                vz_in.at[(*place, halves(half))],
                vz_send.at[place],
                vz_recv.at[place],
                at.z_peer[way],
            )

    joined(0, 4)
    k_step = {(way, way): kz(1, way, way) for way in range(2)}
    va(4)
    va(3)
    va(-3)
    vb(4)
    va(2)
    va(-2)
    k_step = kz_step(k_step, 2)
    vb(3)
    vb(-3)
    vc(4)
    vz(1)
    va(1)
    va(-1)
    vb(2)
    vb(-2)
    vc(3)
    vc(-3)
    vz(2)
    va(0)
    k_step = kz_step(k_step, 3)
    vb(1)
    vb(-1)
    vc(2)
    vc(-2)
    vz(3)
    vb(0)
    vc(1)
    vc(-1)
    vz(4)
    for number, (src, dst) in enumerate([(o_ref, ao_ref), (dq_ref, gq_ref)]):
        for place, (dx, dy) in enumerate(at.offsets):
            xh, y = at.part_of(dx, dy)
            piece = src.at[xh * YN + y]
            slot = dst.at[
                pl.ds(pl.multiple_of(at.xh * HALF, HALF), HALF), lanes(at.y, GROUP * HD)
            ]
            if place == 0:
                move = pltpu.make_async_copy(piece, slot, local.at[number])
            else:
                move = remote(
                    piece,
                    slot,
                    p_send.at[number, place],
                    p_recv.at[number, place],
                    at.part_device(dx, dy),
                )
            move.start()
            moves.append(move)
    k_step = kz_step(k_step, 4)
    vc(0)

    def finish(number, ref):
        for dy in range(YN):
            _, y = at.part_of(0, dy)
            xh, xl = edge(0)
            piece = own.at[number, 3, xh, y, xl]
            slot = ref.at[:, lanes(at.y, HD)]
            if dy == 0:
                move = pltpu.make_async_copy(piece, slot, local.at[2 + number])
            else:
                move = remote(
                    piece,
                    slot,
                    y_send.at[number, dy],
                    y_recv.at[number, dy],
                    at.part_device(0, dy),
                )
            move.start()
            moves.append(move)

    joined(0, 0)
    for half in range(2):
        for way in range(2):
            k_step[half, way].wait_recv()
        where = (0, 3, slice(None), halves(half))
        total = f32(own[where]) + f32(kz_in[0, 3, half]) + f32(kz_in[1, 3, half])
        own[where] = total.astype(jnp.bfloat16)
    first = x_first(0, 0, kx_half, kx_send, kx_recv)
    for way in range(2):
        v_step[way].wait_recv()
    mine = own_chunk(1, 0, 0)
    total = f32(own[mine]) + f32(vz_in[0, 3]) + f32(vz_in[1, 3])
    own[mine] = total.astype(jnp.bfloat16)
    finish(1, gv_ref)
    second = x_second(0, 0, first, kx_half, kx_in, kx_send, kx_recv)
    x_third(0, 0, second, kx_in)
    finish(0, gk_ref)
    for move in moves:
        move.wait()
    for copy in sent:
        copy.wait_send()


def scatter(out, dq, dk, dv):
    tokens = jax.ShapeDtypeStruct((128, QH * HD), jnp.bfloat16)
    pairs = jax.ShapeDtypeStruct((128, KVH * HD), jnp.bfloat16)
    dma = pltpu.SemaphoreType.DMA

    def box(*shape):
        return pltpu.VMEM((*shape, 128, HD), jnp.bfloat16)

    return pl.pallas_call(
        scatter_kernel,
        out_shape=(tokens, tokens, pairs, pairs),
        in_specs=[ANY] * 4,
        out_specs=(ANY,) * 4,
        scratch_shapes=[
            box(2, ZN, XHI, YN, XLO),
            box(2, ZN, XHI, YN, XLO),
            box(2, 4, 2, XHI, 2, XLO),
            box(2, 2),
            box(2, YN),
            box(ZN, 2, 2),
            box(ZN, 2, YN),
            box(2, 4, YN),
            dma((2, ZN)), dma((2, ZN)), dma((2, ZN)), dma((2, 4, 2)), dma((2, 4, 2)),
            dma((2, 2)), dma((2, 2)), dma((2, ZN, 2)), dma((2, ZN, 2)), dma((2, 4)), dma((2, 4)),
            dma((2, PIECES)), dma((2, PIECES)), dma((2, YN)), dma((2, YN)), dma((4,)),
        ],
        compiler_params=pltpu.CompilerParams(
            collective_id=1, has_side_effects=True, vmem_limit_bytes=48 << 20
        ),
        name="scatter",
    )(out, dq, dk.reshape(WHOLE), dv.reshape(WHOLE))


def shards(queries, keys, values, d_out, lengths):
    ka, va, q, g = gather(queries, keys, values, d_out)
    out, dq, dk, dv = attention(lengths, q, g, ka, va)
    return scatter(out, dq, dk, dv)


def solution(mesh):
    spec = P(("ctx", "head"), None)
    return jax.shard_map(
        shards,
        mesh=mesh,
        in_specs=(spec, spec, spec, spec, P()),
        out_specs=(spec,) * 4,
        check_vma=False,
    )
```

```python
import functools
import math

import jax
import jax.numpy as jnp
from jax import lax
from jax.experimental import pallas as pl
from jax.experimental.pallas import tpu as pltpu
from jax.sharding import PartitionSpec as P

QH = 16
KVH = 4
HD = 128
GROUP = QH // KVH
SEQ = 32768
DOC_MOST = 8192
NEG_FILL = -1e30

XHI, XN, YN, ZN, XLO = 2, 4, 4, 8, 2
WHOLE = (XHI, YN, 2, ZN, XLO, 128, 128)
HALF = 64
PIECES = XHI * YN
ROWS = GROUP * HALF
KB = 512
UNITS = 4
KBLOCKS = SEQ // KB
SPAN = (DOC_MOST + HALF - 1 + KB - 1) // KB
FLUSH_SLOTS = 8

MESH = pl.DeviceIdType.MESH
ANY = pl.BlockSpec(memory_space=pl.ANY)
VMEM = pl.BlockSpec(memory_space=pltpu.VMEM)
SMEM = pl.BlockSpec(memory_space=pltpu.SMEM)


def here():
    c = lax.axis_index("ctx")
    h = lax.axis_index("head")
    xh, y, core = c // 8, lax.rem(c // 2, 4), lax.rem(c, 2)
    z, xl = h // 2, lax.rem(h, 2)
    return xh * 2 + xl, y, z, core


def device(x, y, z, core):
    return ((x // 2) * 8 + y * 2 + core, z * 2 + lax.rem(x, 2))


def greet(peers):
    barrier = pltpu.get_barrier_semaphore()
    for peer in peers:
        pl.semaphore_signal(barrier, inc=1, device_id=peer, device_id_type=MESH)
    pl.semaphore_wait(barrier, len(peers))


def remote(src, dst, send, recv, peer):
    return pltpu.make_async_remote_copy(
        src_ref=src, dst_ref=dst, send_sem=send, recv_sem=recv, device_id=peer, device_id_type=MESH
    )


def lanes(start, size):
    return pl.ds(pl.multiple_of(start * size, size), size)


class Spot:
    def __init__(self):
        self.x, self.y, self.z, self.core = here()
        self.xh, self.xl = self.x // 2, lax.rem(self.x, 2)
        self.x_peer = [device(self.x_at(d), self.y, self.z, self.core) for d in (1, -1)]
        self.row_peer = self.x_peer + [device(self.x_at(2), self.y, self.z, self.core)]
        self.z_peer = [device(self.x, self.y, self.z_at(d), self.core) for d in (1, -1)]
        self.partner = device(self.x, self.y, self.z, 1 - self.core)
        self.offsets = [(dx, dy) for dx in range(XHI) for dy in range(YN)]

    def x_at(self, d):
        return lax.rem(self.x + d + XN, XN)

    def z_at(self, d):
        return lax.rem(self.z + d + ZN, ZN)

    def part_of(self, dx, dy):
        return lax.rem(self.xh + dx, XHI), lax.rem(self.y + dy, YN)

    def part_device(self, dx, dy):
        xh, y = self.part_of(dx, dy)
        return device(xh * 2 + self.xl, y, self.z, self.core)

    def peers(self):
        return (
            self.x_peer
            + self.z_peer
            + [self.partner]
            + [self.part_device(dx, dy) for dx, dy in self.offsets[1:]]
        )

    def across_x(self, ref, core, dz, half=None):
        return ref.at[:, halves(half), core, self.z_at(dz)]

    def chunk(self, ref, dx, dz, half=None):
        x = self.x_at(dx)
        return ref.at[x // 2, halves(half), self.core, self.z_at(dz), lax.rem(x, 2)]


def halves(half):
    return pl.ds(0, YN) if half is None else pl.ds(half * 2, 2)


def gather_kernel(
    q_ref, k_ref, v_ref, g_ref, ka_ref, va_ref, qi_ref, gi_ref,
    y_send, y_recv, p_send, p_recv, kx_send, kx_recv, kz_send, kz_recv, vz_send, vz_recv,
    vx_send, vx_recv, c_send, c_recv, local,
):
    at = Spot()
    greet(at.peers())
    copies = []
    for number, (src, dst) in enumerate([(k_ref, ka_ref), (v_ref, va_ref)]):
        slot = dst.at[at.xh, at.y, at.core, at.z, at.xl]
        keep = pltpu.make_async_copy(src.at[:, lanes(at.y, HD)], slot, local.at[number])
        keep.start()
        copies.append([keep])
        for dy in range(1, YN):
            _, y = at.part_of(0, dy)
            send = remote(
                src.at[:, lanes(y, HD)],
                slot,
                y_send.at[number, dy],
                y_recv.at[number, dy],
                at.part_device(0, dy),
            )
            send.start()
            copies[number].append(send)

    sent, crossing = [], []

    def go(piece, send, recv, peer):
        copy = remote(piece, piece, send, recv, peer)
        copy.start()
        sent.append(copy)
        return copy

    def cross(piece):
        number = len(crossing)
        crossing.append(go(piece, c_send.at[number], c_recv.at[number], at.partner))

    def kx(way, piece):
        return go(piece, kx_send.at[way], kx_recv.at[way], at.row_peer[way])

    def kz(step, half, way):
        dz = (1 - step) if way == 0 else (step - 1)
        piece = at.across_x(ka_ref, at.core, dz, half)
        place = (way, step, half)
        return go(piece, kz_send.at[place], kz_recv.at[place], at.z_peer[way])

    def vz(step, way):
        dz = (1 - step) if way == 0 else (step - 1)
        piece = at.chunk(va_ref, 0, dz, way if step == 4 else None)
        return go(piece, vz_send.at[way, step], vz_recv.at[way, step], at.z_peer[way])

    vx_first, vx_second = {}, {}

    def vx(stage, way, dz, piece):
        place = (stage, way, dz + 3)
        return go(piece, vx_send.at[place], vx_recv.at[place], at.x_peer[way])

    def vx_start(dz):
        vx_first[dz] = [vx(0, way, dz, at.chunk(va_ref, 0, dz)) for way in range(2)]

    def vx_forward(dz):
        vx_second[dz] = []
        for way in range(2):
            vx_first[dz][way].wait_recv()
            piece = at.chunk(va_ref, 2 * way - 1, dz, way)
            vx_second[dz].append(vx(1, way, dz, piece))

    def vx_end(dz):
        for copy in vx_second[dz]:
            copy.wait_recv()
        cross(at.across_x(va_ref, at.core, dz))

    def kz_step(before, step):
        after = {}
        for half in range(2):
            for way in range(2):
                if (half, way) not in before:
                    continue
                before[half, way].wait_recv()
                if step < 4 or (step == 4 and half == way):
                    after[half, way] = kz(step, half, way)
                dz = (1 - step) if way == 0 else (step - 1)
                cross(at.across_x(ka_ref, at.core, dz, half))
        return after

    for copy in copies[0]:
        copy.wait()
    k_first = [kx(way, at.chunk(ka_ref, 0, 0)) for way in range(3)]
    for copy in copies[1]:
        copy.wait()
    v_step = [vz(1, way) for way in range(2)]
    vx_start(0)

    def vz_next(step):
        for way in range(2):
            v_step[way].wait_recv()
            v_step[way] = vz(step, way)
            vx_start((1 - step) if way == 0 else (step - 1))

    vz_next(2)
    for copy in k_first:
        copy.wait_recv()
    k_step = {(half, way): kz(1, half, way) for half in range(2) for way in range(2)}
    cross(at.across_x(ka_ref, at.core, 0))
    vz_next(3)
    vx_forward(0)
    vz_next(4)
    k_step = kz_step(k_step, 2)
    vx_forward(-1)
    vx_forward(1)
    vx_end(0)
    for way in range(2):
        v_step[way].wait_recv()
    vx_start(4)
    vx_forward(-2)
    vx_forward(2)
    vx_end(-1)
    vx_end(1)
    k_step = kz_step(k_step, 3)
    moves = []
    for number, (src, dst) in enumerate([(q_ref, qi_ref), (g_ref, gi_ref)]):
        for place, (dx, dy) in enumerate(at.offsets):
            xh, y = at.part_of(dx, dy)
            piece = src.at[pl.ds(pl.multiple_of(xh * HALF, HALF), HALF), lanes(y, GROUP * HD)]
            slot = dst.at[at.xh * YN + at.y]
            if place == 0:
                move = pltpu.make_async_copy(piece, slot, local.at[2 + number])
            else:
                move = remote(
                    piece,
                    slot,
                    p_send.at[number, place],
                    p_recv.at[number, place],
                    at.part_device(dx, dy),
                )
            move.start()
            moves.append(move)

    vx_forward(-3)
    vx_forward(3)
    vx_end(-2)
    vx_end(2)
    k_step = kz_step(k_step, 4)
    vx_forward(4)
    vx_end(-3)
    vx_end(3)
    vx_end(4)
    kz_step(k_step, 5)
    for move in moves:
        move.wait()
    for copy in crossing:
        copy.wait_recv()
    for copy in sent:
        copy.wait_send()


def gather(queries, keys, values, d_out):
    whole = jax.ShapeDtypeStruct(WHOLE, jnp.bfloat16)
    part = jax.ShapeDtypeStruct((PIECES, HALF, GROUP * HD), jnp.bfloat16)
    dma = pltpu.SemaphoreType.DMA
    return pl.pallas_call(
        gather_kernel,
        out_shape=(whole, whole, part, part),
        in_specs=[ANY] * 4,
        out_specs=(ANY,) * 4,
        scratch_shapes=[
            dma((2, YN)), dma((2, YN)), dma((2, PIECES)), dma((2, PIECES)),
            dma((4,)), dma((4,)), dma((2, 5, 2)), dma((2, 5, 2)), dma((2, 5)), dma((2, 5)),
            dma((2, 2, ZN)), dma((2, 2, ZN)), dma((23,)), dma((23,)), dma((4,)),
        ],
        compiler_params=pltpu.CompilerParams(collective_id=0, has_side_effects=True),
        name="gather",
    )(queries, keys, values, d_out)


def attention_kernel(
    meta, first_use, last_use, start_ref, q_ref, g_ref, ka_ref, va_ref, o_ref, dq_ref, dk_ref,
    dv_ref, kbuf, vbuf, sbuf, pbuf, dk_acc, dv_acc, flush, zeros, pending, k_sem, v_sem, f_sem,
    z_sem,
):
    scaling = HD ** (-0.5)
    factor = scaling * math.log2(math.e)

    def block(j, size=KB):
        return pl.ds(pl.multiple_of(j * KB, KB), size)

    def span(low, j, size=KB):
        return pl.ds(pl.multiple_of(low + j * KB, HALF), size)

    def fetches(i, slot, j):
        src = span(meta[i, 0], j)
        return (
            pltpu.make_async_copy(ka_ref.at[src], kbuf.at[slot, block(j)], k_sem.at[slot, j]),
            pltpu.make_async_copy(va_ref.at[src], vbuf.at[slot, block(j)], v_sem.at[slot, j]),
        )

    def fetch(i, slot):
        def body(j, carry):
            for copy in fetches(i, slot, j):
                copy.start()
            return carry

        lax.fori_loop(0, meta[i, 1], body, 0)

    def stacked(value):
        return jnp.concatenate([value[:, h * HD : (h + 1) * HD] for h in range(GROUP)], axis=0)

    def unstacked(value):
        return jnp.concatenate([value[h * HALF : (h + 1) * HALF] for h in range(GROUP)], axis=1)

    def mm(a, b, da, db):
        return lax.dot_general(
            a, b, (((da,), (db,)), ((), ())), preferred_element_type=jnp.float32
        )

    def in_pairs(count, body, carry):
        carry = lax.fori_loop(
            0, count // UNITS, lambda j, c: body(UNITS * j, UNITS * KB, c), carry
        )
        done, units = count // UNITS * UNITS, UNITS // 2
        while units:
            more = lax.rem(count // units, 2)
            carry = lax.cond(
                more == 1,
                lambda c, done=done, units=units: body(done, units * KB, c),
                lambda c: c,
                carry,
            )
            done, units = done + more * units, units // 2
        return carry

    def blanks(kb):
        return (
            pltpu.make_async_copy(zeros, dk_ref.at[block(kb)], z_sem.at[0, kb]),
            pltpu.make_async_copy(zeros, dv_ref.at[block(kb)], z_sem.at[1, kb]),
        )

    def flushes(kb, slot):
        return (
            pltpu.make_async_copy(flush.at[0, slot], dk_ref.at[block(kb)], f_sem.at[0, slot]),
            pltpu.make_async_copy(flush.at[1, slot], dv_ref.at[block(kb)], f_sem.at[1, slot]),
        )

    fetch(0, 0)
    zeros[...] = jnp.zeros((KB, HD), jnp.bfloat16)
    for slot in range(FLUSH_SLOTS):
        pending[slot] = 0

    def blank_start(kb, carry):
        @pl.when(first_use[kb] < 0)
        def _():
            for copy in blanks(kb):
                copy.start()

        return carry

    lax.fori_loop(0, KBLOCKS, blank_start, 0)

    def piece(i, carry):
        slot = lax.rem(i, 2)

        @pl.when(i + 1 < PIECES)
        def _():
            fetch(i + 1, 1 - slot)

        low, count, first, last_start = meta[i, 0], meta[i, 1], meta[i, 2], meta[i, 3]
        q = stacked(q_ref[i])
        g = stacked(g_ref[i])
        starts = start_ref[i]
        times = first + lax.rem(lax.broadcasted_iota(jnp.int32, (1, ROWS), 1), HALF)

        def scores_step(j, size, top):
            for part in range(size // KB):
                fetches(i, slot, j + part)[0].wait()
            base = low + j * KB

            def finish(s):
                sbuf[block(j, size)] = s
                return jnp.maximum(top, jnp.max(s.reshape(size // 8, 8, ROWS), axis=0))

            def scores():
                return mm(kbuf[slot, block(j, size)], q, 1, 1)

            def masked():
                key = lax.broadcasted_iota(jnp.int32, (size, ROWS), 0)
                seen = (key >= starts - base) & (key <= times - base)
                return finish(jnp.where(seen, scores(), NEG_FILL))

            whole = (base >= last_start) & (base + size - 1 <= first)
            return lax.cond(whole, lambda: finish(scores()), masked)

        top = in_pairs(count, scores_step, jnp.full((8, ROWS), NEG_FILL, jnp.float32))
        top = jnp.max(top, axis=0, keepdims=True)

        def weights_step(j, size, carry):
            total, out = carry
            for part in range(size // KB):
                fetches(i, slot, j + part)[1].wait()
            p = jnp.exp2((sbuf[block(j, size)] - top) * factor)
            total = total + jnp.sum(p.reshape(size // 8, 8, ROWS), axis=0)
            p = p.astype(jnp.bfloat16)
            pbuf[block(j, size)] = p
            return total, out + mm(vbuf[slot, block(j, size)], p, 0, 0)

        total, out = in_pairs(
            count,
            weights_step,
            (jnp.zeros((8, ROWS), jnp.float32), jnp.zeros((HD, ROWS), jnp.float32)),
        )
        inverse = 1.0 / jnp.sum(total, axis=0, keepdims=True)
        out = (out * inverse).astype(jnp.bfloat16).astype(jnp.float32)
        o_ref[i] = unstacked(out.T.astype(jnp.bfloat16))
        g_turned = g.astype(jnp.float32).T
        delta = jnp.sum(g_turned * out, axis=0, keepdims=True) * inverse
        g_rows = (g_turned * inverse).T.astype(jnp.bfloat16)
        block_low, block_end = low // KB, (low + count * KB - 1) // KB + 1

        def clear(kb, carry):
            @pl.when(first_use[kb] == i)
            def _():
                dk_acc[block(kb)] = jnp.zeros((KB, HD), jnp.float32)
                dv_acc[block(kb)] = jnp.zeros((KB, HD), jnp.float32)

            return carry

        lax.fori_loop(block_low, block_end, clear, 0)

        def grad_step(j, size, dq):
            k = kbuf[slot, block(j, size)]
            p = pbuf[block(j, size)]
            gp = mm(vbuf[slot, block(j, size)], g_rows, 1, 1)
            ds = (p.astype(jnp.float32) * (gp - delta)).astype(jnp.bfloat16)
            where = span(low, j, size)
            dv_acc[where] += mm(p, g_rows, 1, 0)
            dk_acc[where] += mm(ds, q, 1, 0)
            return dq + mm(k, ds, 0, 0)

        dq = in_pairs(count, grad_step, jnp.zeros((HD, ROWS), jnp.float32))
        dq_ref[i] = unstacked((dq * scaling).T.astype(jnp.bfloat16))

        def flush_step(kb, carry):
            @pl.when(last_use[kb] == i)
            def _():
                slot = lax.rem(kb, FLUSH_SLOTS)

                @pl.when(pending[slot] > 0)
                def _():
                    for copy in flushes(kb, slot):
                        copy.wait()

                pending[slot] = 1
                flush[0, slot] = (dk_acc[block(kb)] * scaling).astype(jnp.bfloat16)
                flush[1, slot] = dv_acc[block(kb)].astype(jnp.bfloat16)
                for copy in flushes(kb, slot):
                    copy.start()

            return carry

        lax.fori_loop(block_low, block_end, flush_step, 0)
        return carry

    lax.fori_loop(0, PIECES, piece, 0)
    for slot in range(FLUSH_SLOTS):

        @pl.when(pending[slot] > 0)
        def _():
            for copy in flushes(0, slot):
                copy.wait()

    def blank_wait(kb, carry):
        @pl.when(first_use[kb] < 0)
        def _():
            for copy in blanks(kb):
                copy.wait()

        return carry

    lax.fori_loop(0, KBLOCKS, blank_wait, 0)


def attention(lengths, q, g, keys, values):
    x, y, z, core = here()
    ends = jnp.cumsum(lengths)
    part = jnp.arange(PIECES, dtype=jnp.int32)
    tile = (part // YN) * 128 + lax.rem(part, YN) * 32 + core * 16 + z * 2 + lax.rem(x, 2)
    first = tile * 128 + (x // 2) * HALF
    times = first[:, None] + jnp.arange(HALF, dtype=jnp.int32)[None, :]
    starts = jnp.sum(
        jnp.where(ends[None, None, :] <= times[:, :, None], lengths[None, None, :], 0), axis=2
    )
    end = first + HALF
    count = (end - starts[:, 0] + KB - 1) // KB
    low = jnp.maximum(end - count * KB, 0)
    meta = jnp.stack([low, count, first, starts[:, HALF - 1]], axis=1).astype(jnp.int32)
    ids = jnp.arange(KBLOCKS, dtype=jnp.int32)[:, None]
    used = (ids >= low[None] // KB) & (ids <= (low + count * KB - 1)[None] // KB)
    last_use = jnp.max(jnp.where(used, part[None], -1), axis=1)
    first_use = jnp.min(jnp.where(used, part[None], PIECES), axis=1)
    first_use = jnp.where(last_use < 0, -1, first_use)
    start_rows = jnp.tile(starts, (1, GROUP)).reshape(PIECES, 1, ROWS).astype(jnp.int32)
    part_shape = jax.ShapeDtypeStruct((PIECES, HALF, GROUP * HD), jnp.bfloat16)
    whole = jax.ShapeDtypeStruct((SEQ, HD), jnp.bfloat16)
    dma = pltpu.SemaphoreType.DMA
    return pl.pallas_call(
        attention_kernel,
        out_shape=(part_shape, part_shape, whole, whole),
        in_specs=[SMEM, SMEM, SMEM, VMEM, VMEM, VMEM, ANY, ANY],
        out_specs=(VMEM, VMEM, ANY, ANY),
        scratch_shapes=[
            pltpu.VMEM((2, SPAN * KB, HD), jnp.bfloat16),
            pltpu.VMEM((2, SPAN * KB, HD), jnp.bfloat16),
            pltpu.VMEM((SPAN * KB, ROWS), jnp.float32),
            pltpu.VMEM((SPAN * KB, ROWS), jnp.bfloat16),
            pltpu.VMEM((SEQ, HD), jnp.float32),
            pltpu.VMEM((SEQ, HD), jnp.float32),
            pltpu.VMEM((2, FLUSH_SLOTS, KB, HD), jnp.bfloat16),
            pltpu.VMEM((KB, HD), jnp.bfloat16),
            pltpu.SMEM((FLUSH_SLOTS,), jnp.int32),
            dma((2, SPAN)),
            dma((2, SPAN)),
            dma((2, FLUSH_SLOTS)),
            dma((2, KBLOCKS)),
        ],
        compiler_params=pltpu.CompilerParams(vmem_limit_bytes=62 << 20),
        name="attention",
    )(
        meta,
        first_use.astype(jnp.int32),
        last_use.astype(jnp.int32),
        start_rows,
        q,
        g,
        keys.reshape(SEQ, HD),
        values.reshape(SEQ, HD),
    )


def scatter_kernel(
    o_ref, dq_ref, dk_ref, dv_ref, ao_ref, gq_ref, gk_ref, gv_ref,
    own, part, kz_in, kx_in, vx_half, vx_in, vz_in,
    own_sem, c_send, c_recv, kz_send, kz_recv, kx_send, kx_recv, vx_send, vx_recv,
    vz_send, vz_recv, p_send, p_recv, y_send, y_recv, local,
):
    at = Spot()
    greet(at.peers())
    ours = [dk_ref, dv_ref]
    sent, moves = [], []

    def go(src, dst, send, recv, peer):
        copy = remote(src, dst, send, recv, peer)
        copy.start()
        sent.append(copy)
        return copy

    waiting = {}
    for dz in (4, 3, -3, 2, -2, 1, -1, 0):
        for number in range(2):
            place = (number, dz + 3)
            load = pltpu.make_async_copy(
                at.across_x(ours[number], at.core, dz), own.at[place], own_sem.at[place]
            )
            load.start()
            theirs = go(
                at.across_x(ours[number], 1 - at.core, dz),
                part.at[place],
                c_send.at[place],
                c_recv.at[place],
                at.partner,
            )
            waiting[number, dz] = (load, theirs)

    def f32(value):
        return value.astype(jnp.float32)

    def joined(number, dz):
        load, theirs = waiting[number, dz]
        load.wait()
        theirs.wait_recv()
        place = (number, dz + 3)
        for xh in range(XHI):
            total = f32(own[(*place, xh)]) + f32(part[(*place, xh)])
            own[(*place, xh)] = total.astype(jnp.bfloat16)

    def add(place, value):
        own[place] = (f32(own[place]) + f32(value)).astype(jnp.bfloat16)

    def kz(step, half, way):
        dz = (5 - step) if way == 0 else (step - 5)
        dz = 4 if dz == -4 else dz
        place = (way, step - 1, half)
        return go(
            own.at[0, dz + 3, :, halves(half)],
            kz_in.at[place],
            kz_send.at[place],
            kz_recv.at[place],
            at.z_peer[way],
        )

    def kz_step(before, step):
        after = {}
        for way in range(2):
            dz = (5 - step) if way == 0 else (step - 5)
            joined(0, dz)
            for half in range(2):
                if (half, way) in before:
                    before[half, way].wait_recv()
                    add((0, dz + 3, slice(None), halves(half)), kz_in[way, step - 2, half])
                after[half, way] = kz(step, half, way)
        return after

    def edge(dx):
        x = at.x_at(dx)
        return x // 2, lax.rem(x, 2)

    def own_chunk(number, dz, dx, half=None):
        xh, xl = edge(dx)
        return (number, dz + 3, xh, halves(half), xl)

    def x_first(number, dz, inbox, send, recv):
        out = []
        for way in range(2):
            place = (dz + 3, way) if number else (way,)
            sem = (0, *place)
            out.append(
                go(
                    own.at[own_chunk(number, dz, 2, way)],
                    inbox.at[place],
                    send.at[sem],
                    recv.at[sem],
                    at.x_peer[way],
                )
            )
        return out

    def x_second(number, dz, first, half_box, inbox, send, recv):
        out = []
        for way in range(2):
            place = (dz + 3, way) if number else (way,)
            sem = (1, *place)
            dx = 1 - 2 * way
            first[way].wait_recv()
            add(own_chunk(number, dz, dx, way), half_box[place])
            out.append(
                go(
                    own.at[own_chunk(number, dz, dx)],
                    inbox.at[place],
                    send.at[sem],
                    recv.at[sem],
                    at.x_peer[way],
                )
            )
        return out

    def x_third(number, dz, second, inbox):
        for way in range(2):
            place = (dz + 3, way) if number else (way,)
            second[way].wait_recv()
        places = [(dz + 3, way) if number else (way,) for way in range(2)]
        mine = own_chunk(number, dz, 0)
        total = f32(own[mine]) + f32(inbox[places[0]]) + f32(inbox[places[1]])
        own[mine] = total.astype(jnp.bfloat16)

    v_first, v_second = {}, {}

    def va(dz):
        joined(1, dz)
        v_first[dz] = x_first(1, dz, vx_half, vx_send, vx_recv)

    def vb(dz):
        v_second[dz] = x_second(1, dz, v_first[dz], vx_half, vx_in, vx_send, vx_recv)

    def vc(dz):
        x_third(1, dz, v_second[dz], vx_in)

    v_step = [None, None]

    def vz(step):
        for way in range(2):
            dz = (5 - step) if way == 0 else (step - 5)
            dz = 4 if dz == -4 else dz
            half = way if step == 1 else None
            if step == 2:
                v_step[way].wait_recv()
                add(own_chunk(1, dz, 0, way), vz_in[way, 0, halves(way)])
            elif step > 2:
                v_step[way].wait_recv()
                add(own_chunk(1, dz, 0), vz_in[way, step - 2])
            place = (way, step - 1)
            v_step[way] = go(
                own.at[own_chunk(1, dz, 0, half)],
                vz_in.at[(*place, halves(half))],
                vz_send.at[place],
                vz_recv.at[place],
                at.z_peer[way],
            )

    joined(0, 4)
    k_step = {(way, way): kz(1, way, way) for way in range(2)}
    va(4)
    va(3)
    va(-3)
    vb(4)
    va(2)
    va(-2)
    k_step = kz_step(k_step, 2)
    vb(3)
    vb(-3)
    vc(4)
    vz(1)
    va(1)
    va(-1)
    vb(2)
    vb(-2)
    vc(3)
    vc(-3)
    vz(2)
    va(0)
    k_step = kz_step(k_step, 3)
    vb(1)
    vb(-1)
    vc(2)
    vc(-2)
    vz(3)
    vb(0)
    vc(1)
    vc(-1)
    vz(4)
    for number, (src, dst) in enumerate([(o_ref, ao_ref), (dq_ref, gq_ref)]):
        for place, (dx, dy) in enumerate(at.offsets):
            xh, y = at.part_of(dx, dy)
            piece = src.at[xh * YN + y]
            slot = dst.at[
                pl.ds(pl.multiple_of(at.xh * HALF, HALF), HALF), lanes(at.y, GROUP * HD)
            ]
            if place == 0:
                move = pltpu.make_async_copy(piece, slot, local.at[number])
            else:
                move = remote(
                    piece,
                    slot,
                    p_send.at[number, place],
                    p_recv.at[number, place],
                    at.part_device(dx, dy),
                )
            move.start()
            moves.append(move)
    k_step = kz_step(k_step, 4)
    vc(0)

    def finish(number, ref):
        for dy in range(YN):
            _, y = at.part_of(0, dy)
            xh, xl = edge(0)
            piece = own.at[number, 3, xh, y, xl]
            slot = ref.at[:, lanes(at.y, HD)]
            if dy == 0:
                move = pltpu.make_async_copy(piece, slot, local.at[2 + number])
            else:
                move = remote(
                    piece,
                    slot,
                    y_send.at[number, dy],
                    y_recv.at[number, dy],
                    at.part_device(0, dy),
                )
            move.start()
            moves.append(move)

    joined(0, 0)
    for half in range(2):
        for way in range(2):
            k_step[half, way].wait_recv()
        where = (0, 3, slice(None), halves(half))
        total = f32(own[where]) + f32(kz_in[0, 3, half]) + f32(kz_in[1, 3, half])
        own[where] = total.astype(jnp.bfloat16)
    row = [
        go(
            own.at[own_chunk(0, 0, dx)],
            kx_in.at[way],
            kx_send.at[way],
            kx_recv.at[way],
            at.row_peer[way],
        )
        for way, dx in enumerate((1, -1, 2))
    ]
    for way in range(2):
        v_step[way].wait_recv()
    mine = own_chunk(1, 0, 0)
    total = f32(own[mine]) + f32(vz_in[0, 3]) + f32(vz_in[1, 3])
    own[mine] = total.astype(jnp.bfloat16)
    finish(1, gv_ref)
    mine = own_chunk(0, 0, 0)
    total = f32(own[mine])
    for way in range(3):
        row[way].wait_recv()
        total = total + f32(kx_in[way])
    own[mine] = total.astype(jnp.bfloat16)
    finish(0, gk_ref)
    for move in moves:
        move.wait()
    for copy in sent:
        copy.wait_send()


def scatter(out, dq, dk, dv):
    tokens = jax.ShapeDtypeStruct((128, QH * HD), jnp.bfloat16)
    pairs = jax.ShapeDtypeStruct((128, KVH * HD), jnp.bfloat16)
    dma = pltpu.SemaphoreType.DMA

    def box(*shape):
        return pltpu.VMEM((*shape, 128, HD), jnp.bfloat16)

    return pl.pallas_call(
        scatter_kernel,
        out_shape=(tokens, tokens, pairs, pairs),
        in_specs=[ANY] * 4,
        out_specs=(ANY,) * 4,
        scratch_shapes=[
            box(2, ZN, XHI, YN, XLO),
            box(2, ZN, XHI, YN, XLO),
            box(2, 4, 2, XHI, 2, XLO),
            box(3, YN),
            box(ZN, 2, 2),
            box(ZN, 2, YN),
            box(2, 4, YN),
            dma((2, ZN)), dma((2, ZN)), dma((2, ZN)), dma((2, 4, 2)), dma((2, 4, 2)),
            dma((3,)), dma((3,)), dma((2, ZN, 2)), dma((2, ZN, 2)), dma((2, 4)), dma((2, 4)),
            dma((2, PIECES)), dma((2, PIECES)), dma((2, YN)), dma((2, YN)), dma((4,)),
        ],
        compiler_params=pltpu.CompilerParams(
            collective_id=1, has_side_effects=True, vmem_limit_bytes=48 << 20
        ),
        name="scatter",
    )(out, dq, dk.reshape(WHOLE), dv.reshape(WHOLE))


def shards(queries, keys, values, d_out, lengths):
    ka, va, q, g = gather(queries, keys, values, d_out)
    out, dq, dk, dv = attention(lengths, q, g, ka, va)
    return scatter(out, dq, dk, dv)


def solution(mesh):
    spec = P(("ctx", "head"), None)
    return jax.shard_map(
        shards,
        mesh=mesh,
        in_specs=(spec, spec, spec, spec, P()),
        out_specs=(spec,) * 4,
        check_vma=False,
    )
```

```python
import functools
import math

import jax
import jax.numpy as jnp
from jax import lax
from jax.experimental import pallas as pl
from jax.experimental.pallas import tpu as pltpu
from jax.sharding import PartitionSpec as P

QH = 16
KVH = 4
HD = 128
GROUP = QH // KVH
SEQ = 32768
DOC_MOST = 8192
NEG_FILL = -1e30

XHI, XN, YN, ZN, XLO = 2, 4, 4, 8, 2
WHOLE = (XHI, YN, 2, ZN, XLO, 128, 128)
HALF = 64
PIECES = XHI * YN
ROWS = GROUP * HALF
KB = 512
UNITS = 4
KBLOCKS = SEQ // KB
SPAN = (DOC_MOST + HALF - 1 + KB - 1) // KB
FLUSH_SLOTS = 8

MESH = pl.DeviceIdType.MESH
ANY = pl.BlockSpec(memory_space=pl.ANY)
VMEM = pl.BlockSpec(memory_space=pltpu.VMEM)
SMEM = pl.BlockSpec(memory_space=pltpu.SMEM)


def here():
    c = lax.axis_index("ctx")
    h = lax.axis_index("head")
    xh, y, core = c // 8, lax.rem(c // 2, 4), lax.rem(c, 2)
    z, xl = h // 2, lax.rem(h, 2)
    return xh * 2 + xl, y, z, core


def device(x, y, z, core):
    return ((x // 2) * 8 + y * 2 + core, z * 2 + lax.rem(x, 2))


def greet(peers):
    barrier = pltpu.get_barrier_semaphore()
    for peer in peers:
        pl.semaphore_signal(barrier, inc=1, device_id=peer, device_id_type=MESH)
    pl.semaphore_wait(barrier, len(peers))


def remote(src, dst, send, recv, peer):
    return pltpu.make_async_remote_copy(
        src_ref=src, dst_ref=dst, send_sem=send, recv_sem=recv, device_id=peer, device_id_type=MESH
    )


def lanes(start, size):
    return pl.ds(pl.multiple_of(start * size, size), size)


class Spot:
    def __init__(self):
        self.x, self.y, self.z, self.core = here()
        self.xh, self.xl = self.x // 2, lax.rem(self.x, 2)
        self.x_peer = [device(self.x_at(d), self.y, self.z, self.core) for d in (1, -1)]
        self.row_peer = self.x_peer + [device(self.x_at(2), self.y, self.z, self.core)]
        self.z_peer = [device(self.x, self.y, self.z_at(d), self.core) for d in (1, -1)]
        self.partner = device(self.x, self.y, self.z, 1 - self.core)
        self.offsets = [(dx, dy) for dx in range(XHI) for dy in range(YN)]

    def x_at(self, d):
        return lax.rem(self.x + d + XN, XN)

    def z_at(self, d):
        return lax.rem(self.z + d + ZN, ZN)

    def part_of(self, dx, dy):
        return lax.rem(self.xh + dx, XHI), lax.rem(self.y + dy, YN)

    def part_device(self, dx, dy):
        xh, y = self.part_of(dx, dy)
        return device(xh * 2 + self.xl, y, self.z, self.core)

    def peers(self):
        return (
            self.x_peer
            + self.z_peer
            + [self.partner]
            + [self.part_device(dx, dy) for dx, dy in self.offsets[1:]]
        )

    def across_x(self, ref, core, dz, half=None):
        return ref.at[:, halves(half), core, self.z_at(dz)]

    def chunk(self, ref, dx, dz, half=None):
        x = self.x_at(dx)
        return ref.at[x // 2, halves(half), self.core, self.z_at(dz), lax.rem(x, 2)]


def halves(half):
    return pl.ds(0, YN) if half is None else pl.ds(half * 2, 2)


def gather_kernel(
    q_ref, k_ref, v_ref, g_ref, ka_ref, va_ref, qi_ref, gi_ref,
    y_send, y_recv, p_send, p_recv, kx_send, kx_recv, kz_send, kz_recv, vz_send, vz_recv,
    vx_send, vx_recv, c_send, c_recv, local,
):
    at = Spot()
    greet(at.peers())
    copies = []
    for number, (src, dst) in enumerate([(k_ref, ka_ref), (v_ref, va_ref)]):
        slot = dst.at[at.xh, at.y, at.core, at.z, at.xl]
        keep = pltpu.make_async_copy(src.at[:, lanes(at.y, HD)], slot, local.at[number])
        keep.start()
        copies.append([keep])
        for dy in range(1, YN):
            _, y = at.part_of(0, dy)
            send = remote(
                src.at[:, lanes(y, HD)],
                slot,
                y_send.at[number, dy],
                y_recv.at[number, dy],
                at.part_device(0, dy),
            )
            send.start()
            copies[number].append(send)

    sent, crossing = [], []

    def go(piece, send, recv, peer):
        copy = remote(piece, piece, send, recv, peer)
        copy.start()
        sent.append(copy)
        return copy

    def cross(piece):
        number = len(crossing)
        crossing.append(go(piece, c_send.at[number], c_recv.at[number], at.partner))

    def kx(way, piece):
        return go(piece, kx_send.at[way], kx_recv.at[way], at.row_peer[way])

    def kz(step, half, way):
        dz = (1 - step) if way == 0 else (step - 1)
        piece = at.across_x(ka_ref, at.core, dz, half)
        place = (way, step, half)
        return go(piece, kz_send.at[place], kz_recv.at[place], at.z_peer[way])

    def vz(step, way):
        dz = (1 - step) if way == 0 else (step - 1)
        piece = at.chunk(va_ref, 0, dz, way if step == 4 else None)
        return go(piece, vz_send.at[way, step], vz_recv.at[way, step], at.z_peer[way])

    vx_first, vx_second = {}, {}

    def vx(stage, way, dz, piece):
        place = (stage, way, dz + 3)
        return go(piece, vx_send.at[place], vx_recv.at[place], at.x_peer[way])

    def vx_start(dz):
        vx_first[dz] = [vx(0, way, dz, at.chunk(va_ref, 0, dz)) for way in range(2)]

    def vx_forward(dz):
        vx_second[dz] = []
        for way in range(2):
            vx_first[dz][way].wait_recv()
            piece = at.chunk(va_ref, 2 * way - 1, dz, way)
            vx_second[dz].append(vx(1, way, dz, piece))

    def vx_end(dz):
        for copy in vx_second[dz]:
            copy.wait_recv()
        cross(at.across_x(va_ref, at.core, dz))

    def kz_step(before, step):
        after = {}
        for half in range(2):
            for way in range(2):
                if (half, way) not in before:
                    continue
                before[half, way].wait_recv()
                if step < 4 or (step == 4 and half == way):
                    after[half, way] = kz(step, half, way)
                dz = (1 - step) if way == 0 else (step - 1)
                cross(at.across_x(ka_ref, at.core, dz, half))
        return after

    for copy in copies[0]:
        copy.wait()
    k_first = [kx(way, at.chunk(ka_ref, 0, 0)) for way in range(3)]
    for copy in copies[1]:
        copy.wait()
    v_step = [vz(1, way) for way in range(2)]
    vx_start(0)

    def vz_next(step):
        for way in range(2):
            v_step[way].wait_recv()
            v_step[way] = vz(step, way)
            vx_start((1 - step) if way == 0 else (step - 1))

    vz_next(2)
    for copy in k_first:
        copy.wait_recv()
    k_step = {(half, way): kz(1, half, way) for half in range(2) for way in range(2)}
    cross(at.across_x(ka_ref, at.core, 0))
    vz_next(3)
    vx_forward(0)
    vz_next(4)
    k_step = kz_step(k_step, 2)
    vx_forward(-1)
    vx_forward(1)
    vx_end(0)
    for way in range(2):
        v_step[way].wait_recv()
    vx_start(4)
    vx_forward(-2)
    vx_forward(2)
    vx_end(-1)
    vx_end(1)
    k_step = kz_step(k_step, 3)
    moves = []
    for number, (src, dst) in enumerate([(q_ref, qi_ref), (g_ref, gi_ref)]):
        for place, (dx, dy) in enumerate(at.offsets):
            xh, y = at.part_of(dx, dy)
            piece = src.at[pl.ds(pl.multiple_of(xh * HALF, HALF), HALF), lanes(y, GROUP * HD)]
            slot = dst.at[at.xh * YN + at.y]
            if place == 0:
                move = pltpu.make_async_copy(piece, slot, local.at[2 + number])
            else:
                move = remote(
                    piece,
                    slot,
                    p_send.at[number, place],
                    p_recv.at[number, place],
                    at.part_device(dx, dy),
                )
            move.start()
            moves.append(move)

    vx_forward(-3)
    vx_forward(3)
    vx_end(-2)
    vx_end(2)
    k_step = kz_step(k_step, 4)
    vx_forward(4)
    vx_end(-3)
    vx_end(3)
    vx_end(4)
    kz_step(k_step, 5)
    for move in moves:
        move.wait()
    for copy in crossing:
        copy.wait_recv()
    for copy in sent:
        copy.wait_send()


def gather(queries, keys, values, d_out):
    whole = jax.ShapeDtypeStruct(WHOLE, jnp.bfloat16)
    part = jax.ShapeDtypeStruct((PIECES, HALF, GROUP * HD), jnp.bfloat16)
    dma = pltpu.SemaphoreType.DMA
    return pl.pallas_call(
        gather_kernel,
        out_shape=(whole, whole, part, part),
        in_specs=[ANY] * 4,
        out_specs=(ANY,) * 4,
        scratch_shapes=[
            dma((2, YN)), dma((2, YN)), dma((2, PIECES)), dma((2, PIECES)),
            dma((4,)), dma((4,)), dma((2, 5, 2)), dma((2, 5, 2)), dma((2, 5)), dma((2, 5)),
            dma((2, 2, ZN)), dma((2, 2, ZN)), dma((23,)), dma((23,)), dma((4,)),
        ],
        compiler_params=pltpu.CompilerParams(collective_id=0, has_side_effects=True),
        name="gather",
    )(queries, keys, values, d_out)


def attention_kernel(
    meta, start_ref, q_ref, g_ref, ka_ref, va_ref, o_ref, dq_ref, dk_ref, dv_ref,
    kbuf, vbuf, sbuf, pbuf, dk_acc, dv_acc, flush, zeros, result, pending, first_use, last_use,
    k_sem, v_sem, f_sem, z_sem, o_sem,
):
    scaling = HD ** (-0.5)
    factor = scaling * math.log2(math.e)

    def block(j, size=KB):
        return pl.ds(pl.multiple_of(j * KB, KB), size)

    def span(low, j, size=KB):
        return pl.ds(pl.multiple_of(low + j * KB, HALF), size)

    def fetches(i, slot, j):
        src = span(meta[i, 0], j)
        return (
            pltpu.make_async_copy(ka_ref.at[src], kbuf.at[slot, block(j)], k_sem.at[slot, j]),
            pltpu.make_async_copy(va_ref.at[src], vbuf.at[slot, block(j)], v_sem.at[slot, j]),
        )

    def fetch(i, slot):
        def body(j, carry):
            for copy in fetches(i, slot, j):
                copy.start()
            return carry

        lax.fori_loop(0, meta[i, 1], body, 0)

    def stacked(value):
        return jnp.concatenate([value[:, h * HD : (h + 1) * HD] for h in range(GROUP)], axis=0)

    def unstacked(value):
        return jnp.concatenate([value[h * HALF : (h + 1) * HALF] for h in range(GROUP)], axis=1)

    def mm(a, b, da, db):
        return lax.dot_general(
            a, b, (((da,), (db,)), ((), ())), preferred_element_type=jnp.float32
        )

    def in_pairs(count, body, carry):
        carry = lax.fori_loop(
            0, count // UNITS, lambda j, c: body(UNITS * j, UNITS * KB, c), carry
        )
        done, units = count // UNITS * UNITS, UNITS // 2
        while units:
            more = lax.rem(count // units, 2)
            carry = lax.cond(
                more == 1,
                lambda c, done=done, units=units: body(done, units * KB, c),
                lambda c: c,
                carry,
            )
            done, units = done + more * units, units // 2
        return carry

    def blanks(kb):
        return (
            pltpu.make_async_copy(zeros, dk_ref.at[block(kb)], z_sem.at[0, kb]),
            pltpu.make_async_copy(zeros, dv_ref.at[block(kb)], z_sem.at[1, kb]),
        )

    def flushes(kb, slot):
        return (
            pltpu.make_async_copy(flush.at[0, slot], dk_ref.at[block(kb)], f_sem.at[0, slot]),
            pltpu.make_async_copy(flush.at[1, slot], dv_ref.at[block(kb)], f_sem.at[1, slot]),
        )

    def results(i, slot):
        return (
            pltpu.make_async_copy(result.at[0, slot], o_ref.at[i], o_sem.at[0, slot]),
            pltpu.make_async_copy(result.at[1, slot], dq_ref.at[i], o_sem.at[1, slot]),
        )

    def blocks_of(i):
        low, count = meta[i, 0], meta[i, 1]
        return low // KB, (low + count * KB - 1) // KB + 1

    fetch(0, 0)

    def unused(kb, carry):
        first_use[kb] = -1
        last_use[kb] = -1
        return carry

    lax.fori_loop(0, KBLOCKS, unused, 0)

    def mark_piece(i, carry):
        def mark(kb, carry):
            last_use[kb] = i
            seen = first_use[kb]
            first_use[kb] = jnp.where(seen < 0, i, seen)
            return carry

        lax.fori_loop(*blocks_of(i), mark, 0)
        return carry

    lax.fori_loop(0, PIECES, mark_piece, 0)
    zeros[...] = jnp.zeros((KB, HD), jnp.bfloat16)
    for slot in range(FLUSH_SLOTS):
        pending[slot] = 0

    def blank_start(kb, carry):
        @pl.when(first_use[kb] < 0)
        def _():
            for copy in blanks(kb):
                copy.start()

        return carry

    lax.fori_loop(0, KBLOCKS, blank_start, 0)

    def piece(i, carry):
        slot = lax.rem(i, 2)

        @pl.when(i + 1 < PIECES)
        def _():
            fetch(i + 1, 1 - slot)

        low, count, first, last_start = meta[i, 0], meta[i, 1], meta[i, 2], meta[i, 3]
        q = stacked(q_ref[i])
        g = stacked(g_ref[i])
        starts = start_ref[i]
        times = first + lax.rem(lax.broadcasted_iota(jnp.int32, (1, ROWS), 1), HALF)

        def scores_step(j, size, top):
            for part in range(size // KB):
                fetches(i, slot, j + part)[0].wait()
            base = low + j * KB

            def finish(s):
                sbuf[block(j, size)] = s
                return jnp.maximum(top, jnp.max(s.reshape(size // 8, 8, ROWS), axis=0))

            def scores():
                return mm(kbuf[slot, block(j, size)], q, 1, 1)

            def masked():
                key = lax.broadcasted_iota(jnp.int32, (size, ROWS), 0)
                seen = (key >= starts - base) & (key <= times - base)
                return finish(jnp.where(seen, scores(), NEG_FILL))

            whole = (base >= last_start) & (base + size - 1 <= first)
            return lax.cond(whole, lambda: finish(scores()), masked)

        top = in_pairs(count, scores_step, jnp.full((8, ROWS), NEG_FILL, jnp.float32))
        top = jnp.max(top, axis=0, keepdims=True)

        def weights_step(j, size, carry):
            total, out = carry
            for part in range(size // KB):
                fetches(i, slot, j + part)[1].wait()
            p = jnp.exp2((sbuf[block(j, size)] - top) * factor)
            total = total + jnp.sum(p.reshape(size // 8, 8, ROWS), axis=0)
            p = p.astype(jnp.bfloat16)
            pbuf[block(j, size)] = p
            return total, out + mm(vbuf[slot, block(j, size)], p, 0, 0)

        total, out = in_pairs(
            count,
            weights_step,
            (jnp.zeros((8, ROWS), jnp.float32), jnp.zeros((HD, ROWS), jnp.float32)),
        )
        inverse = 1.0 / jnp.sum(total, axis=0, keepdims=True)
        out = (out * inverse).astype(jnp.bfloat16).astype(jnp.float32)

        @pl.when(i >= 2)
        def _():
            for copy in results(i - 2, slot):
                copy.wait()

        result[0, slot] = unstacked(out.T.astype(jnp.bfloat16))
        g_turned = g.astype(jnp.float32).T
        delta = jnp.sum(g_turned * out, axis=0, keepdims=True) * inverse
        g_rows = (g_turned * inverse).T.astype(jnp.bfloat16)
        block_low, block_end = blocks_of(i)

        def clear(kb, carry):
            @pl.when(first_use[kb] == i)
            def _():
                dk_acc[block(kb)] = jnp.zeros((KB, HD), jnp.float32)
                dv_acc[block(kb)] = jnp.zeros((KB, HD), jnp.float32)

            return carry

        lax.fori_loop(block_low, block_end, clear, 0)

        def grad_step(j, size, dq):
            k = kbuf[slot, block(j, size)]
            p = pbuf[block(j, size)]
            gp = mm(vbuf[slot, block(j, size)], g_rows, 1, 1)
            ds = (p.astype(jnp.float32) * (gp - delta)).astype(jnp.bfloat16)
            where = span(low, j, size)
            dv_acc[where] += mm(p, g_rows, 1, 0)
            dk_acc[where] += mm(ds, q, 1, 0)
            return dq + mm(k, ds, 0, 0)

        dq = in_pairs(count, grad_step, jnp.zeros((HD, ROWS), jnp.float32))
        result[1, slot] = unstacked((dq * scaling).T.astype(jnp.bfloat16))
        for copy in results(i, slot):
            copy.start()

        def flush_step(kb, carry):
            @pl.when(last_use[kb] == i)
            def _():
                slot = lax.rem(kb, FLUSH_SLOTS)

                @pl.when(pending[slot] > 0)
                def _():
                    for copy in flushes(kb, slot):
                        copy.wait()

                pending[slot] = 1
                flush[0, slot] = (dk_acc[block(kb)] * scaling).astype(jnp.bfloat16)
                flush[1, slot] = dv_acc[block(kb)].astype(jnp.bfloat16)
                for copy in flushes(kb, slot):
                    copy.start()

            return carry

        lax.fori_loop(block_low, block_end, flush_step, 0)
        return carry

    lax.fori_loop(0, PIECES, piece, 0)
    for i in (PIECES - 2, PIECES - 1):
        for copy in results(i, i % 2):
            copy.wait()
    for slot in range(FLUSH_SLOTS):

        @pl.when(pending[slot] > 0)
        def _():
            for copy in flushes(0, slot):
                copy.wait()

    def blank_wait(kb, carry):
        @pl.when(first_use[kb] < 0)
        def _():
            for copy in blanks(kb):
                copy.wait()

        return carry

    lax.fori_loop(0, KBLOCKS, blank_wait, 0)


def attention(lengths, q, g, keys, values):
    x, y, z, core = here()
    ends = jnp.cumsum(lengths)
    part = jnp.arange(PIECES, dtype=jnp.int32)
    tile = (part // YN) * 128 + lax.rem(part, YN) * 32 + core * 16 + z * 2 + lax.rem(x, 2)
    first = tile * 128 + (x // 2) * HALF
    times = first[:, None] + lax.rem(jnp.arange(ROWS, dtype=jnp.int32), HALF)[None, :]
    starts = jnp.sum(
        jnp.where(ends[None, None, :] <= times[:, :, None], lengths[None, None, :], 0), axis=2
    )
    end = first + HALF
    count = (end - starts[:, 0] + KB - 1) // KB
    low = jnp.maximum(end - count * KB, 0)
    meta = jnp.stack([low, count, first, starts[:, HALF - 1]], axis=1).astype(jnp.int32)
    start_rows = starts.reshape(PIECES, 1, ROWS).astype(jnp.int32)
    part_shape = jax.ShapeDtypeStruct((PIECES, HALF, GROUP * HD), jnp.bfloat16)
    whole = jax.ShapeDtypeStruct((SEQ, HD), jnp.bfloat16)
    dma = pltpu.SemaphoreType.DMA
    return pl.pallas_call(
        attention_kernel,
        out_shape=(part_shape, part_shape, whole, whole),
        in_specs=[SMEM, VMEM, VMEM, VMEM, ANY, ANY],
        out_specs=(ANY,) * 4,
        scratch_shapes=[
            pltpu.VMEM((2, SPAN * KB, HD), jnp.bfloat16),
            pltpu.VMEM((2, SPAN * KB, HD), jnp.bfloat16),
            pltpu.VMEM((SPAN * KB, ROWS), jnp.float32),
            pltpu.VMEM((SPAN * KB, ROWS), jnp.bfloat16),
            pltpu.VMEM((SEQ, HD), jnp.float32),
            pltpu.VMEM((SEQ, HD), jnp.float32),
            pltpu.VMEM((2, FLUSH_SLOTS, KB, HD), jnp.bfloat16),
            pltpu.VMEM((KB, HD), jnp.bfloat16),
            pltpu.VMEM((2, 2, HALF, GROUP * HD), jnp.bfloat16),
            pltpu.SMEM((FLUSH_SLOTS,), jnp.int32),
            pltpu.SMEM((KBLOCKS,), jnp.int32),
            pltpu.SMEM((KBLOCKS,), jnp.int32),
            dma((2, SPAN)),
            dma((2, SPAN)),
            dma((2, FLUSH_SLOTS)),
            dma((2, KBLOCKS)),
            dma((2, 2)),
        ],
        compiler_params=pltpu.CompilerParams(vmem_limit_bytes=62 << 20),
        name="attention",
    )(
        meta,
        start_rows,
        q,
        g,
        keys.reshape(SEQ, HD),
        values.reshape(SEQ, HD),
    )


def scatter_kernel(
    o_ref, dq_ref, dk_ref, dv_ref, ao_ref, gq_ref, gk_ref, gv_ref,
    own, part, kz_in, kx_in, vx_half, vx_in, vz_in,
    own_sem, c_send, c_recv, kz_send, kz_recv, kx_send, kx_recv, vx_send, vx_recv,
    vz_send, vz_recv, p_send, p_recv, y_send, y_recv, local,
):
    at = Spot()
    greet(at.peers())
    ours = [dk_ref, dv_ref]
    sent, moves = [], []

    def go(src, dst, send, recv, peer):
        copy = remote(src, dst, send, recv, peer)
        copy.start()
        sent.append(copy)
        return copy

    waiting = {}
    for dz in (4, 3, -3, 2, -2, 1, -1, 0):
        for number in range(2):
            place = (number, dz + 3)
            load = pltpu.make_async_copy(
                at.across_x(ours[number], at.core, dz), own.at[place], own_sem.at[place]
            )
            load.start()
            theirs = go(
                at.across_x(ours[number], 1 - at.core, dz),
                part.at[place],
                c_send.at[place],
                c_recv.at[place],
                at.partner,
            )
            waiting[number, dz] = (load, theirs)

    def f32(value):
        return value.astype(jnp.float32)

    def joined(number, dz):
        load, theirs = waiting[number, dz]
        load.wait()
        theirs.wait_recv()
        place = (number, dz + 3)
        for xh in range(XHI):
            total = f32(own[(*place, xh)]) + f32(part[(*place, xh)])
            own[(*place, xh)] = total.astype(jnp.bfloat16)

    def add(place, value):
        own[place] = (f32(own[place]) + f32(value)).astype(jnp.bfloat16)

    def kz(step, half, way):
        dz = (5 - step) if way == 0 else (step - 5)
        dz = 4 if dz == -4 else dz
        place = (way, step - 1, half)
        return go(
            own.at[0, dz + 3, :, halves(half)],
            kz_in.at[place],
            kz_send.at[place],
            kz_recv.at[place],
            at.z_peer[way],
        )

    def kz_step(before, step):
        after = {}
        for way in range(2):
            dz = (5 - step) if way == 0 else (step - 5)
            joined(0, dz)
            for half in range(2):
                if (half, way) in before:
                    before[half, way].wait_recv()
                    add((0, dz + 3, slice(None), halves(half)), kz_in[way, step - 2, half])
                after[half, way] = kz(step, half, way)
        return after

    def edge(dx):
        x = at.x_at(dx)
        return x // 2, lax.rem(x, 2)

    def own_chunk(number, dz, dx, half=None):
        xh, xl = edge(dx)
        return (number, dz + 3, xh, halves(half), xl)

    def x_first(number, dz, inbox, send, recv):
        out = []
        for way in range(2):
            place = (dz + 3, way) if number else (way,)
            sem = (0, *place)
            out.append(
                go(
                    own.at[own_chunk(number, dz, 2, way)],
                    inbox.at[place],
                    send.at[sem],
                    recv.at[sem],
                    at.x_peer[way],
                )
            )
        return out

    def x_second(number, dz, first, half_box, inbox, send, recv):
        out = []
        for way in range(2):
            place = (dz + 3, way) if number else (way,)
            sem = (1, *place)
            dx = 1 - 2 * way
            first[way].wait_recv()
            add(own_chunk(number, dz, dx, way), half_box[place])
            out.append(
                go(
                    own.at[own_chunk(number, dz, dx)],
                    inbox.at[place],
                    send.at[sem],
                    recv.at[sem],
                    at.x_peer[way],
                )
            )
        return out

    def x_third(number, dz, second, inbox):
        for way in range(2):
            place = (dz + 3, way) if number else (way,)
            second[way].wait_recv()
        places = [(dz + 3, way) if number else (way,) for way in range(2)]
        mine = own_chunk(number, dz, 0)
        total = f32(own[mine]) + f32(inbox[places[0]]) + f32(inbox[places[1]])
        own[mine] = total.astype(jnp.bfloat16)

    v_first, v_second = {}, {}

    def va(dz):
        joined(1, dz)
        v_first[dz] = x_first(1, dz, vx_half, vx_send, vx_recv)

    def vb(dz):
        v_second[dz] = x_second(1, dz, v_first[dz], vx_half, vx_in, vx_send, vx_recv)

    def vc(dz):
        x_third(1, dz, v_second[dz], vx_in)

    v_step = [None, None]

    def vz(step):
        for way in range(2):
            dz = (5 - step) if way == 0 else (step - 5)
            dz = 4 if dz == -4 else dz
            half = way if step == 1 else None
            if step == 2:
                v_step[way].wait_recv()
                add(own_chunk(1, dz, 0, way), vz_in[way, 0, halves(way)])
            elif step > 2:
                v_step[way].wait_recv()
                add(own_chunk(1, dz, 0), vz_in[way, step - 2])
            place = (way, step - 1)
            v_step[way] = go(
                own.at[own_chunk(1, dz, 0, half)],
                vz_in.at[(*place, halves(half))],
                vz_send.at[place],
                vz_recv.at[place],
                at.z_peer[way],
            )

    joined(0, 4)
    k_step = {(way, way): kz(1, way, way) for way in range(2)}
    va(4)
    va(3)
    va(-3)
    vb(4)
    va(2)
    va(-2)
    k_step = kz_step(k_step, 2)
    vb(3)
    vb(-3)
    vc(4)
    vz(1)
    va(1)
    va(-1)
    vb(2)
    vb(-2)
    vc(3)
    vc(-3)
    vz(2)
    va(0)
    k_step = kz_step(k_step, 3)
    vb(1)
    vb(-1)
    vc(2)
    vc(-2)
    vz(3)
    vb(0)
    vc(1)
    vc(-1)
    vz(4)
    for number, (src, dst) in enumerate([(o_ref, ao_ref), (dq_ref, gq_ref)]):
        for place, (dx, dy) in enumerate(at.offsets):
            xh, y = at.part_of(dx, dy)
            piece = src.at[xh * YN + y]
            slot = dst.at[
                pl.ds(pl.multiple_of(at.xh * HALF, HALF), HALF), lanes(at.y, GROUP * HD)
            ]
            if place == 0:
                move = pltpu.make_async_copy(piece, slot, local.at[number])
            else:
                move = remote(
                    piece,
                    slot,
                    p_send.at[number, place],
                    p_recv.at[number, place],
                    at.part_device(dx, dy),
                )
            move.start()
            moves.append(move)
    k_step = kz_step(k_step, 4)
    vc(0)

    def finish(number, ref):
        for dy in range(YN):
            _, y = at.part_of(0, dy)
            xh, xl = edge(0)
            piece = own.at[number, 3, xh, y, xl]
            slot = ref.at[:, lanes(at.y, HD)]
            if dy == 0:
                move = pltpu.make_async_copy(piece, slot, local.at[2 + number])
            else:
                move = remote(
                    piece,
                    slot,
                    y_send.at[number, dy],
                    y_recv.at[number, dy],
                    at.part_device(0, dy),
                )
            move.start()
            moves.append(move)

    joined(0, 0)
    for half in range(2):
        for way in range(2):
            k_step[half, way].wait_recv()
        where = (0, 3, slice(None), halves(half))
        total = f32(own[where]) + f32(kz_in[0, 3, half]) + f32(kz_in[1, 3, half])
        own[where] = total.astype(jnp.bfloat16)
    row = [
        go(
            own.at[own_chunk(0, 0, dx)],
            kx_in.at[way],
            kx_send.at[way],
            kx_recv.at[way],
            at.row_peer[way],
        )
        for way, dx in enumerate((1, -1, 2))
    ]
    for way in range(2):
        v_step[way].wait_recv()
    mine = own_chunk(1, 0, 0)
    total = f32(own[mine]) + f32(vz_in[0, 3]) + f32(vz_in[1, 3])
    own[mine] = total.astype(jnp.bfloat16)
    finish(1, gv_ref)
    mine = own_chunk(0, 0, 0)
    total = f32(own[mine])
    for way in range(3):
        row[way].wait_recv()
        total = total + f32(kx_in[way])
    own[mine] = total.astype(jnp.bfloat16)
    finish(0, gk_ref)
    for move in moves:
        move.wait()
    for copy in sent:
        copy.wait_send()


def scatter(out, dq, dk, dv):
    tokens = jax.ShapeDtypeStruct((128, QH * HD), jnp.bfloat16)
    pairs = jax.ShapeDtypeStruct((128, KVH * HD), jnp.bfloat16)
    dma = pltpu.SemaphoreType.DMA

    def box(*shape):
        return pltpu.VMEM((*shape, 128, HD), jnp.bfloat16)

    return pl.pallas_call(
        scatter_kernel,
        out_shape=(tokens, tokens, pairs, pairs),
        in_specs=[ANY] * 4,
        out_specs=(ANY,) * 4,
        scratch_shapes=[
            box(2, ZN, XHI, YN, XLO),
            box(2, ZN, XHI, YN, XLO),
            box(2, 4, 2, XHI, 2, XLO),
            box(3, YN),
            box(ZN, 2, 2),
            box(ZN, 2, YN),
            box(2, 4, YN),
            dma((2, ZN)), dma((2, ZN)), dma((2, ZN)), dma((2, 4, 2)), dma((2, 4, 2)),
            dma((3,)), dma((3,)), dma((2, ZN, 2)), dma((2, ZN, 2)), dma((2, 4)), dma((2, 4)),
            dma((2, PIECES)), dma((2, PIECES)), dma((2, YN)), dma((2, YN)), dma((4,)),
        ],
        compiler_params=pltpu.CompilerParams(
            collective_id=1, has_side_effects=True, vmem_limit_bytes=48 << 20
        ),
        name="scatter",
    )(out, dq, dk.reshape(WHOLE), dv.reshape(WHOLE))


def shards(queries, keys, values, d_out, lengths):
    ka, va, q, g = gather(queries, keys, values, d_out)
    out, dq, dk, dv = attention(lengths, q, g, ka, va)
    return scatter(out, dq, dk, dv)


def solution(mesh):
    spec = P(("ctx", "head"), None)
    return jax.shard_map(
        shards,
        mesh=mesh,
        in_specs=(spec, spec, spec, spec, P()),
        out_specs=(spec,) * 4,
        check_vma=False,
    )
```

```python
import functools
import math

import jax
import jax.numpy as jnp
from jax import lax
from jax.experimental import pallas as pl
from jax.experimental.pallas import tpu as pltpu
from jax.sharding import PartitionSpec as P

QH = 16
KVH = 4
HD = 128
GROUP = QH // KVH
SEQ = 32768
DOC_MOST = 8192
NEG_FILL = -1e30

XHI, XN, YN, ZN, XLO = 2, 4, 4, 8, 2
WHOLE = (XHI, YN, 2, ZN, XLO, 128, 128)
HALF = 64
PIECES = XHI * YN
ROWS = GROUP * HALF
KB = 512
UNITS = 4
KBLOCKS = SEQ // KB
SPAN = (DOC_MOST + HALF - 1 + KB - 1) // KB
FLUSH_SLOTS = 8

MESH = pl.DeviceIdType.MESH
ANY = pl.BlockSpec(memory_space=pl.ANY)
VMEM = pl.BlockSpec(memory_space=pltpu.VMEM)
SMEM = pl.BlockSpec(memory_space=pltpu.SMEM)


def here():
    c = lax.axis_index("ctx")
    h = lax.axis_index("head")
    xh, y, core = c // 8, lax.rem(c // 2, 4), lax.rem(c, 2)
    z, xl = h // 2, lax.rem(h, 2)
    return xh * 2 + xl, y, z, core


def device(x, y, z, core):
    return ((x // 2) * 8 + y * 2 + core, z * 2 + lax.rem(x, 2))


def greet(peers):
    barrier = pltpu.get_barrier_semaphore()
    for peer in peers:
        pl.semaphore_signal(barrier, inc=1, device_id=peer, device_id_type=MESH)
    pl.semaphore_wait(barrier, len(peers))


def remote(src, dst, send, recv, peer):
    return pltpu.make_async_remote_copy(
        src_ref=src, dst_ref=dst, send_sem=send, recv_sem=recv, device_id=peer, device_id_type=MESH
    )


def lanes(start, size):
    return pl.ds(pl.multiple_of(start * size, size), size)


class Spot:
    def __init__(self):
        self.x, self.y, self.z, self.core = here()
        self.xh, self.xl = self.x // 2, lax.rem(self.x, 2)
        self.x_peer = [device(self.x_at(d), self.y, self.z, self.core) for d in (1, -1)]
        self.row_peer = self.x_peer + [device(self.x_at(2), self.y, self.z, self.core)]
        self.z_peer = [device(self.x, self.y, self.z_at(d), self.core) for d in (1, -1)]
        self.partner = device(self.x, self.y, self.z, 1 - self.core)
        self.offsets = [(dx, dy) for dx in range(XHI) for dy in range(YN)]

    def x_at(self, d):
        return lax.rem(self.x + d + XN, XN)

    def z_at(self, d):
        return lax.rem(self.z + d + ZN, ZN)

    def part_of(self, dx, dy):
        return lax.rem(self.xh + dx, XHI), lax.rem(self.y + dy, YN)

    def part_device(self, dx, dy):
        xh, y = self.part_of(dx, dy)
        return device(xh * 2 + self.xl, y, self.z, self.core)

    def peers(self):
        return (
            self.x_peer
            + self.z_peer
            + [self.partner]
            + [self.part_device(dx, dy) for dx, dy in self.offsets[1:]]
        )

    def across_x(self, ref, core, dz, half=None):
        return ref.at[:, halves(half), core, self.z_at(dz)]

    def chunk(self, ref, dx, dz, half=None):
        x = self.x_at(dx)
        return ref.at[x // 2, halves(half), self.core, self.z_at(dz), lax.rem(x, 2)]


def halves(half):
    return pl.ds(0, YN) if half is None else pl.ds(half * 2, 2)


def gather_kernel(
    q_ref, k_ref, v_ref, g_ref, ka_ref, va_ref, qi_ref, gi_ref,
    y_send, y_recv, p_send, p_recv, kx_send, kx_recv, kz_send, kz_recv, vz_send, vz_recv,
    vx_send, vx_recv, c_send, c_recv, local,
):
    at = Spot()
    greet(at.peers())
    copies = []
    for number, (src, dst) in enumerate([(k_ref, ka_ref), (v_ref, va_ref)]):
        slot = dst.at[at.xh, at.y, at.core, at.z, at.xl]
        keep = pltpu.make_async_copy(src.at[:, lanes(at.y, HD)], slot, local.at[number])
        keep.start()
        copies.append([keep])
        for dy in range(1, YN):
            _, y = at.part_of(0, dy)
            send = remote(
                src.at[:, lanes(y, HD)],
                slot,
                y_send.at[number, dy],
                y_recv.at[number, dy],
                at.part_device(0, dy),
            )
            send.start()
            copies[number].append(send)

    sent, crossing = [], []

    def go(piece, send, recv, peer):
        copy = remote(piece, piece, send, recv, peer)
        copy.start()
        sent.append(copy)
        return copy

    def cross(piece):
        number = len(crossing)
        crossing.append(go(piece, c_send.at[number], c_recv.at[number], at.partner))

    def kx(way, piece):
        return go(piece, kx_send.at[way], kx_recv.at[way], at.row_peer[way])

    def kz(step, half, way):
        dz = (1 - step) if way == 0 else (step - 1)
        piece = at.across_x(ka_ref, at.core, dz, half)
        place = (way, step, half)
        return go(piece, kz_send.at[place], kz_recv.at[place], at.z_peer[way])

    def vz(step, way):
        dz = (1 - step) if way == 0 else (step - 1)
        piece = at.chunk(va_ref, 0, dz, way if step == 4 else None)
        return go(piece, vz_send.at[way, step], vz_recv.at[way, step], at.z_peer[way])

    vx_first, vx_second = {}, {}

    def vx(stage, way, dz, piece):
        place = (stage, way, dz + 3)
        return go(piece, vx_send.at[place], vx_recv.at[place], at.x_peer[way])

    def vx_start(dz):
        vx_first[dz] = [vx(0, way, dz, at.chunk(va_ref, 0, dz)) for way in range(2)]

    def vx_forward(dz):
        vx_second[dz] = []
        for way in range(2):
            vx_first[dz][way].wait_recv()
            piece = at.chunk(va_ref, 2 * way - 1, dz, way)
            vx_second[dz].append(vx(1, way, dz, piece))

    def vx_end(dz):
        for copy in vx_second[dz]:
            copy.wait_recv()
        cross(at.across_x(va_ref, at.core, dz))

    def kz_step(before, step):
        after = {}
        for half in range(2):
            for way in range(2):
                if (half, way) not in before:
                    continue
                before[half, way].wait_recv()
                if step < 4 or (step == 4 and half == way):
                    after[half, way] = kz(step, half, way)
                dz = (1 - step) if way == 0 else (step - 1)
                cross(at.across_x(ka_ref, at.core, dz, half))
        return after

    for copy in copies[0]:
        copy.wait()
    k_first = [kx(way, at.chunk(ka_ref, 0, 0)) for way in range(3)]
    for copy in copies[1]:
        copy.wait()
    v_step = [vz(1, way) for way in range(2)]
    vx_start(0)

    def vz_next(step):
        for way in range(2):
            v_step[way].wait_recv()
            v_step[way] = vz(step, way)
            vx_start((1 - step) if way == 0 else (step - 1))

    vz_next(2)
    for copy in k_first:
        copy.wait_recv()
    k_step = {(half, way): kz(1, half, way) for half in range(2) for way in range(2)}
    cross(at.across_x(ka_ref, at.core, 0))
    vz_next(3)
    vx_forward(0)
    vz_next(4)
    k_step = kz_step(k_step, 2)
    vx_forward(-1)
    vx_forward(1)
    vx_end(0)
    for way in range(2):
        v_step[way].wait_recv()
    vx_start(4)
    vx_forward(-2)
    vx_forward(2)
    vx_end(-1)
    vx_end(1)
    k_step = kz_step(k_step, 3)
    moves = []
    for number, (src, dst) in enumerate([(q_ref, qi_ref), (g_ref, gi_ref)]):
        for place, (dx, dy) in enumerate(at.offsets):
            xh, y = at.part_of(dx, dy)
            piece = src.at[pl.ds(pl.multiple_of(xh * HALF, HALF), HALF), lanes(y, GROUP * HD)]
            slot = dst.at[at.xh * YN + at.y]
            if place == 0:
                move = pltpu.make_async_copy(piece, slot, local.at[2 + number])
            else:
                move = remote(
                    piece,
                    slot,
                    p_send.at[number, place],
                    p_recv.at[number, place],
                    at.part_device(dx, dy),
                )
            move.start()
            moves.append(move)

    vx_forward(-3)
    vx_forward(3)
    vx_end(-2)
    vx_end(2)
    k_step = kz_step(k_step, 4)
    vx_forward(4)
    vx_end(-3)
    vx_end(3)
    vx_end(4)
    kz_step(k_step, 5)
    for move in moves:
        move.wait()
    for copy in crossing:
        copy.wait_recv()
    for copy in sent:
        copy.wait_send()


def gather(queries, keys, values, d_out):
    whole = jax.ShapeDtypeStruct(WHOLE, jnp.bfloat16)
    part = jax.ShapeDtypeStruct((PIECES, HALF, GROUP * HD), jnp.bfloat16)
    dma = pltpu.SemaphoreType.DMA
    return pl.pallas_call(
        gather_kernel,
        out_shape=(whole, whole, part, part),
        in_specs=[ANY] * 4,
        out_specs=(ANY,) * 4,
        scratch_shapes=[
            dma((2, YN)), dma((2, YN)), dma((2, PIECES)), dma((2, PIECES)),
            dma((4,)), dma((4,)), dma((2, 5, 2)), dma((2, 5, 2)), dma((2, 5)), dma((2, 5)),
            dma((2, 2, ZN)), dma((2, 2, ZN)), dma((23,)), dma((23,)), dma((4,)),
        ],
        compiler_params=pltpu.CompilerParams(collective_id=0, has_side_effects=True),
        name="gather",
    )(queries, keys, values, d_out)


def attention_kernel(
    meta, start_ref, q_ref, g_ref, ka_ref, va_ref, o_ref, dq_ref, dk_ref, dv_ref,
    kbuf, vbuf, sbuf, pbuf, dk_acc, dv_acc, flush, zeros, result, pending, first_use, last_use,
    k_sem, v_sem, f_sem, z_sem, o_sem,
):
    scaling = HD ** (-0.5)
    factor = scaling * math.log2(math.e)

    def block(j, size=KB):
        return pl.ds(pl.multiple_of(j * KB, KB), size)

    def span(low, j, size=KB):
        return pl.ds(pl.multiple_of(low + j * KB, HALF), size)

    def fetches(i, slot, j):
        src = span(meta[i, 0], j)
        return (
            pltpu.make_async_copy(ka_ref.at[src], kbuf.at[slot, block(j)], k_sem.at[slot, j]),
            pltpu.make_async_copy(va_ref.at[src], vbuf.at[slot, block(j)], v_sem.at[slot, j]),
        )

    def fetch(i, slot):
        def body(j, carry):
            for copy in fetches(i, slot, j):
                copy.start()
            return carry

        lax.fori_loop(0, meta[i, 1], body, 0)

    def stacked(value):
        return jnp.concatenate([value[:, h * HD : (h + 1) * HD] for h in range(GROUP)], axis=0)

    def unstacked(value):
        return jnp.concatenate([value[h * HALF : (h + 1) * HALF] for h in range(GROUP)], axis=1)

    def mm(a, b, da, db):
        return lax.dot_general(
            a, b, (((da,), (db,)), ((), ())), preferred_element_type=jnp.float32
        )

    def in_pairs(count, body, carry):
        carry = lax.fori_loop(
            0, count // UNITS, lambda j, c: body(UNITS * j, UNITS * KB, c), carry
        )
        done, units = count // UNITS * UNITS, UNITS // 2
        while units:
            more = lax.rem(count // units, 2)
            carry = lax.cond(
                more == 1,
                lambda c, done=done, units=units: body(done, units * KB, c),
                lambda c: c,
                carry,
            )
            done, units = done + more * units, units // 2
        return carry

    def blanks(kb):
        return (
            pltpu.make_async_copy(zeros, dk_ref.at[block(kb)], z_sem.at[0, kb]),
            pltpu.make_async_copy(zeros, dv_ref.at[block(kb)], z_sem.at[1, kb]),
        )

    def flushes(kb, slot):
        return (
            pltpu.make_async_copy(flush.at[0, slot], dk_ref.at[block(kb)], f_sem.at[0, slot]),
            pltpu.make_async_copy(flush.at[1, slot], dv_ref.at[block(kb)], f_sem.at[1, slot]),
        )

    def results(i, slot):
        return (
            pltpu.make_async_copy(result.at[0, slot], o_ref.at[i], o_sem.at[0, slot]),
            pltpu.make_async_copy(result.at[1, slot], dq_ref.at[i], o_sem.at[1, slot]),
        )

    def blocks_of(i):
        low, count = meta[i, 0], meta[i, 1]
        return low // KB, (low + count * KB - 1) // KB + 1

    fetch(0, 0)

    def unused(kb, carry):
        first_use[kb] = -1
        last_use[kb] = -1
        return carry

    lax.fori_loop(0, KBLOCKS, unused, 0)

    def mark_piece(i, carry):
        def mark(kb, carry):
            last_use[kb] = i
            seen = first_use[kb]
            first_use[kb] = jnp.where(seen < 0, i, seen)
            return carry

        lax.fori_loop(*blocks_of(i), mark, 0)
        return carry

    lax.fori_loop(0, PIECES, mark_piece, 0)
    zeros[...] = jnp.zeros((KB, HD), jnp.bfloat16)
    for slot in range(FLUSH_SLOTS):
        pending[slot] = 0

    def blank_start(kb, carry):
        @pl.when(first_use[kb] < 0)
        def _():
            for copy in blanks(kb):
                copy.start()

        return carry

    lax.fori_loop(0, KBLOCKS, blank_start, 0)

    def piece(i, carry):
        slot = lax.rem(i, 2)

        @pl.when(i + 1 < PIECES)
        def _():
            fetch(i + 1, 1 - slot)

        low, count, first, last_start = meta[i, 0], meta[i, 1], meta[i, 2], meta[i, 3]
        q = stacked(q_ref[i])
        g = stacked(g_ref[i])
        starts = start_ref[i]
        times = first + lax.rem(lax.broadcasted_iota(jnp.int32, (1, ROWS), 1), HALF)

        def scores_step(j, size, top):
            for part in range(size // KB):
                fetches(i, slot, j + part)[0].wait()
            base = low + j * KB

            def finish(s):
                sbuf[block(j, size)] = s
                return jnp.maximum(top, jnp.max(s.reshape(size // 8, 8, ROWS), axis=0))

            def scores():
                return mm(kbuf[slot, block(j, size)], q, 1, 1)

            def masked():
                key = lax.broadcasted_iota(jnp.int32, (size, ROWS), 0)
                seen = (key >= starts - base) & (key <= times - base)
                return finish(jnp.where(seen, scores(), NEG_FILL))

            whole = (base >= last_start) & (base + size - 1 <= first)
            return lax.cond(whole, lambda: finish(scores()), masked)

        top = in_pairs(count, scores_step, jnp.full((8, ROWS), NEG_FILL, jnp.float32))
        top = jnp.max(top, axis=0, keepdims=True)

        def weights_step(j, size, carry):
            total, out = carry
            for part in range(size // KB):
                fetches(i, slot, j + part)[1].wait()
            p = jnp.exp2((sbuf[block(j, size)] - top) * factor)
            total = total + jnp.sum(p.reshape(size // 8, 8, ROWS), axis=0)
            p = p.astype(jnp.bfloat16)
            pbuf[block(j, size)] = p
            return total, out + mm(vbuf[slot, block(j, size)], p, 0, 0)

        total, out = in_pairs(
            count,
            weights_step,
            (jnp.zeros((8, ROWS), jnp.float32), jnp.zeros((HD, ROWS), jnp.float32)),
        )
        inverse = 1.0 / jnp.sum(total, axis=0, keepdims=True)
        out = (out * inverse).astype(jnp.bfloat16).astype(jnp.float32)

        @pl.when(i >= 2)
        def _():
            for copy in results(i - 2, slot):
                copy.wait()

        result[0, slot] = unstacked(out.T.astype(jnp.bfloat16))
        g_turned = g.astype(jnp.float32).T
        delta = jnp.sum(g_turned * out, axis=0, keepdims=True) * inverse
        g_rows = (g_turned * inverse).T.astype(jnp.bfloat16)
        block_low, block_end = blocks_of(i)

        def clear(kb, carry):
            @pl.when(first_use[kb] == i)
            def _():
                dk_acc[block(kb)] = jnp.zeros((KB, HD), jnp.float32)
                dv_acc[block(kb)] = jnp.zeros((KB, HD), jnp.float32)

            return carry

        lax.fori_loop(block_low, block_end, clear, 0)

        def grad_step(j, size, dq):
            k = kbuf[slot, block(j, size)]
            p = pbuf[block(j, size)]
            gp = mm(vbuf[slot, block(j, size)], g_rows, 1, 1)
            ds = (p.astype(jnp.float32) * (gp - delta)).astype(jnp.bfloat16)
            where = span(low, j, size)
            dv_acc[where] += mm(p, g_rows, 1, 0)
            dk_acc[where] += mm(ds, q, 1, 0)
            return dq + mm(k, ds, 0, 0)

        dq = in_pairs(count, grad_step, jnp.zeros((HD, ROWS), jnp.float32))
        result[1, slot] = unstacked((dq * scaling).T.astype(jnp.bfloat16))
        for copy in results(i, slot):
            copy.start()

        def flush_step(kb, carry):
            @pl.when(last_use[kb] == i)
            def _():
                slot = lax.rem(kb, FLUSH_SLOTS)

                @pl.when(pending[slot] > 0)
                def _():
                    for copy in flushes(kb, slot):
                        copy.wait()

                pending[slot] = 1
                flush[0, slot] = (dk_acc[block(kb)] * scaling).astype(jnp.bfloat16)
                flush[1, slot] = dv_acc[block(kb)].astype(jnp.bfloat16)
                for copy in flushes(kb, slot):
                    copy.start()

            return carry

        lax.fori_loop(block_low, block_end, flush_step, 0)
        return carry

    lax.fori_loop(0, PIECES, piece, 0)
    for i in (PIECES - 2, PIECES - 1):
        for copy in results(i, i % 2):
            copy.wait()
    for slot in range(FLUSH_SLOTS):

        @pl.when(pending[slot] > 0)
        def _():
            for copy in flushes(0, slot):
                copy.wait()

    def blank_wait(kb, carry):
        @pl.when(first_use[kb] < 0)
        def _():
            for copy in blanks(kb):
                copy.wait()

        return carry

    lax.fori_loop(0, KBLOCKS, blank_wait, 0)


def attention(lengths, q, g, keys, values):
    x, y, z, core = here()
    ends = jnp.cumsum(lengths)
    part = jnp.arange(PIECES, dtype=jnp.int32)
    tile = (part // YN) * 128 + lax.rem(part, YN) * 32 + core * 16 + z * 2 + lax.rem(x, 2)
    first = tile * 128 + (x // 2) * HALF
    times = first[:, None] + lax.rem(jnp.arange(ROWS, dtype=jnp.int32), HALF)[None, :]
    starts = jnp.sum(
        jnp.where(ends[None, None, :] <= times[:, :, None], lengths[None, None, :], 0), axis=2
    )
    end = first + HALF
    count = (end - starts[:, 0] + KB - 1) // KB
    low = jnp.maximum(end - count * KB, 0)
    meta = jnp.stack([low, count, first, starts[:, HALF - 1]], axis=1).astype(jnp.int32)
    start_rows = starts.reshape(PIECES, 1, ROWS).astype(jnp.int32)
    part_shape = jax.ShapeDtypeStruct((PIECES, HALF, GROUP * HD), jnp.bfloat16)
    whole = jax.ShapeDtypeStruct((SEQ, HD), jnp.bfloat16)
    dma = pltpu.SemaphoreType.DMA
    return pl.pallas_call(
        attention_kernel,
        out_shape=(part_shape, part_shape, whole, whole),
        in_specs=[SMEM, VMEM, VMEM, VMEM, ANY, ANY],
        out_specs=(ANY,) * 4,
        scratch_shapes=[
            pltpu.VMEM((2, SPAN * KB, HD), jnp.bfloat16),
            pltpu.VMEM((2, SPAN * KB, HD), jnp.bfloat16),
            pltpu.VMEM((SPAN * KB, ROWS), jnp.float32),
            pltpu.VMEM((SPAN * KB, ROWS), jnp.bfloat16),
            pltpu.VMEM((SEQ, HD), jnp.float32),
            pltpu.VMEM((SEQ, HD), jnp.float32),
            pltpu.VMEM((2, FLUSH_SLOTS, KB, HD), jnp.bfloat16),
            pltpu.VMEM((KB, HD), jnp.bfloat16),
            pltpu.VMEM((2, 2, HALF, GROUP * HD), jnp.bfloat16),
            pltpu.SMEM((FLUSH_SLOTS,), jnp.int32),
            pltpu.SMEM((KBLOCKS,), jnp.int32),
            pltpu.SMEM((KBLOCKS,), jnp.int32),
            dma((2, SPAN)),
            dma((2, SPAN)),
            dma((2, FLUSH_SLOTS)),
            dma((2, KBLOCKS)),
            dma((2, 2)),
        ],
        compiler_params=pltpu.CompilerParams(vmem_limit_bytes=62 << 20),
        name="attention",
    )(
        meta,
        start_rows,
        q,
        g,
        keys.reshape(SEQ, HD),
        values.reshape(SEQ, HD),
    )


def scatter_kernel(
    o_ref, dq_ref, dk_ref, dv_ref, ao_ref, gq_ref, gk_ref, gv_ref,
    own, part, kz_in, kx_in, vx_half, vx_in, vz_in,
    own_sem, c_send, c_recv, kz_send, kz_recv, kx_send, kx_recv, vx_send, vx_recv,
    vz_send, vz_recv, p_send, p_recv, y_send, y_recv, local,
):
    at = Spot()
    greet(at.peers())
    ours = [dk_ref, dv_ref]
    sent, moves = [], []

    def go(src, dst, send, recv, peer):
        copy = remote(src, dst, send, recv, peer)
        copy.start()
        sent.append(copy)
        return copy

    waiting = {}
    for dz in (4, 3, -3, 2, -2, 1, -1, 0):
        for number in range(2):
            place = (number, dz + 3)
            load = pltpu.make_async_copy(
                at.across_x(ours[number], at.core, dz), own.at[place], own_sem.at[place]
            )
            load.start()
            theirs = go(
                at.across_x(ours[number], 1 - at.core, dz),
                part.at[place],
                c_send.at[place],
                c_recv.at[place],
                at.partner,
            )
            waiting[number, dz] = (load, theirs)

    def f32(value):
        return value.astype(jnp.float32)

    def joined(number, dz):
        load, theirs = waiting[number, dz]
        load.wait()
        theirs.wait_recv()
        place = (number, dz + 3)
        for xh in range(XHI):
            total = f32(own[(*place, xh)]) + f32(part[(*place, xh)])
            own[(*place, xh)] = total.astype(jnp.bfloat16)

    def add(place, value):
        own[place] = (f32(own[place]) + f32(value)).astype(jnp.bfloat16)

    def kz(step, half, way):
        dz = (5 - step) if way == 0 else (step - 5)
        dz = 4 if dz == -4 else dz
        place = (way, step - 1, half)
        return go(
            own.at[0, dz + 3, :, halves(half)],
            kz_in.at[place],
            kz_send.at[place],
            kz_recv.at[place],
            at.z_peer[way],
        )

    def kz_step(before, step):
        after = {}
        for way in range(2):
            dz = (5 - step) if way == 0 else (step - 5)
            joined(0, dz)
            for half in range(2):
                if (half, way) in before:
                    before[half, way].wait_recv()
                    add((0, dz + 3, slice(None), halves(half)), kz_in[way, step - 2, half])
                after[half, way] = kz(step, half, way)
        return after

    def edge(dx):
        x = at.x_at(dx)
        return x // 2, lax.rem(x, 2)

    def own_chunk(number, dz, dx, half=None):
        xh, xl = edge(dx)
        return (number, dz + 3, xh, halves(half), xl)

    def x_first(number, dz, inbox, send, recv):
        out = []
        for way in range(2):
            place = (dz + 3, way) if number else (way,)
            sem = (0, *place)
            out.append(
                go(
                    own.at[own_chunk(number, dz, 2, way)],
                    inbox.at[place],
                    send.at[sem],
                    recv.at[sem],
                    at.x_peer[way],
                )
            )
        return out

    def x_second(number, dz, first, half_box, inbox, send, recv):
        out = []
        for way in range(2):
            place = (dz + 3, way) if number else (way,)
            sem = (1, *place)
            dx = 1 - 2 * way
            first[way].wait_recv()
            add(own_chunk(number, dz, dx, way), half_box[place])
            out.append(
                go(
                    own.at[own_chunk(number, dz, dx)],
                    inbox.at[place],
                    send.at[sem],
                    recv.at[sem],
                    at.x_peer[way],
                )
            )
        return out

    def x_third(number, dz, second, inbox):
        for way in range(2):
            place = (dz + 3, way) if number else (way,)
            second[way].wait_recv()
        places = [(dz + 3, way) if number else (way,) for way in range(2)]
        mine = own_chunk(number, dz, 0)
        total = f32(own[mine]) + f32(inbox[places[0]]) + f32(inbox[places[1]])
        own[mine] = total.astype(jnp.bfloat16)

    v_first, v_second = {}, {}

    def va(dz):
        joined(1, dz)
        v_first[dz] = x_first(1, dz, vx_half, vx_send, vx_recv)

    def vb(dz):
        v_second[dz] = x_second(1, dz, v_first[dz], vx_half, vx_in, vx_send, vx_recv)

    def vc(dz):
        x_third(1, dz, v_second[dz], vx_in)

    v_step = [None, None]

    def vz(step):
        for way in range(2):
            dz = (5 - step) if way == 0 else (step - 5)
            dz = 4 if dz == -4 else dz
            half = way if step == 1 else None
            if step == 2:
                v_step[way].wait_recv()
                add(own_chunk(1, dz, 0, way), vz_in[way, 0, halves(way)])
            elif step > 2:
                v_step[way].wait_recv()
                add(own_chunk(1, dz, 0), vz_in[way, step - 2])
            place = (way, step - 1)
            v_step[way] = go(
                own.at[own_chunk(1, dz, 0, half)],
                vz_in.at[(*place, halves(half))],
                vz_send.at[place],
                vz_recv.at[place],
                at.z_peer[way],
            )

    joined(0, 4)
    k_step = {(way, way): kz(1, way, way) for way in range(2)}
    va(4)
    va(3)
    va(-3)
    vb(4)
    va(2)
    va(-2)
    k_step = kz_step(k_step, 2)
    vb(3)
    vb(-3)
    vc(4)
    vz(1)
    va(1)
    va(-1)
    vb(2)
    vb(-2)
    vc(3)
    vc(-3)
    vz(2)
    va(0)
    k_step = kz_step(k_step, 3)
    vb(1)
    vb(-1)
    vc(2)
    vc(-2)
    vz(3)
    vb(0)
    vc(1)
    vc(-1)
    vz(4)
    for number, (src, dst) in enumerate([(o_ref, ao_ref), (dq_ref, gq_ref)]):
        for place, (dx, dy) in enumerate(at.offsets):
            xh, y = at.part_of(dx, dy)
            piece = src.at[xh * YN + y]
            slot = dst.at[
                pl.ds(pl.multiple_of(at.xh * HALF, HALF), HALF), lanes(at.y, GROUP * HD)
            ]
            if place == 0:
                move = pltpu.make_async_copy(piece, slot, local.at[number])
            else:
                move = remote(
                    piece,
                    slot,
                    p_send.at[number, place],
                    p_recv.at[number, place],
                    at.part_device(dx, dy),
                )
            move.start()
            moves.append(move)
    k_step = kz_step(k_step, 4)
    vc(0)

    def finish(number, ref):
        for dy in range(YN):
            _, y = at.part_of(0, dy)
            xh, xl = edge(0)
            piece = own.at[number, 3, xh, y, xl]
            slot = ref.at[:, lanes(at.y, HD)]
            if dy == 0:
                move = pltpu.make_async_copy(piece, slot, local.at[2 + number])
            else:
                move = remote(
                    piece,
                    slot,
                    y_send.at[number, dy],
                    y_recv.at[number, dy],
                    at.part_device(0, dy),
                )
            move.start()
            moves.append(move)

    joined(0, 0)
    for half in range(2):
        for way in range(2):
            k_step[half, way].wait_recv()
        where = (0, 3, slice(None), halves(half))
        total = f32(own[where]) + f32(kz_in[0, 3, half]) + f32(kz_in[1, 3, half])
        own[where] = total.astype(jnp.bfloat16)
    row = [
        go(
            own.at[own_chunk(0, 0, dx)],
            kx_in.at[way],
            kx_send.at[way],
            kx_recv.at[way],
            at.row_peer[way],
        )
        for way, dx in enumerate((1, -1, 2))
    ]
    for way in range(2):
        v_step[way].wait_recv()
    mine = own_chunk(1, 0, 0)
    total = f32(own[mine]) + f32(vz_in[0, 3]) + f32(vz_in[1, 3])
    own[mine] = total.astype(jnp.bfloat16)
    finish(1, gv_ref)
    mine = own_chunk(0, 0, 0)
    total = f32(own[mine])
    for way in range(3):
        row[way].wait_recv()
        total = total + f32(kx_in[way])
    own[mine] = total.astype(jnp.bfloat16)
    finish(0, gk_ref)
    for move in moves:
        move.wait()
    for copy in sent:
        copy.wait_send()


def scatter(out, dq, dk, dv):
    tokens = jax.ShapeDtypeStruct((128, QH * HD), jnp.bfloat16)
    pairs = jax.ShapeDtypeStruct((128, KVH * HD), jnp.bfloat16)
    dma = pltpu.SemaphoreType.DMA

    def box(*shape):
        return pltpu.VMEM((*shape, 128, HD), jnp.bfloat16)

    return pl.pallas_call(
        scatter_kernel,
        out_shape=(tokens, tokens, pairs, pairs),
        in_specs=[ANY] * 4,
        out_specs=(ANY,) * 4,
        scratch_shapes=[
            box(2, ZN, XHI, YN, XLO),
            box(2, ZN, XHI, YN, XLO),
            box(2, 4, 2, XHI, 2, XLO),
            box(3, YN),
            box(ZN, 2, 2),
            box(ZN, 2, YN),
            box(2, 4, YN),
            dma((2, ZN)), dma((2, ZN)), dma((2, ZN)), dma((2, 4, 2)), dma((2, 4, 2)),
            dma((3,)), dma((3,)), dma((2, ZN, 2)), dma((2, ZN, 2)), dma((2, 4)), dma((2, 4)),
            dma((2, PIECES)), dma((2, PIECES)), dma((2, YN)), dma((2, YN)), dma((4,)),
        ],
        compiler_params=pltpu.CompilerParams(
            collective_id=1, has_side_effects=True, vmem_limit_bytes=63 << 20
        ),
        name="scatter",
    )(out, dq, dk.reshape(WHOLE), dv.reshape(WHOLE))


def shards(queries, keys, values, d_out, lengths):
    ka, va, q, g = gather(queries, keys, values, d_out)
    out, dq, dk, dv = attention(lengths, q, g, ka, va)
    return scatter(out, dq, dk, dv)


def solution(mesh):
    spec = P(("ctx", "head"), None)
    return jax.shard_map(
        shards,
        mesh=mesh,
        in_specs=(spec, spec, spec, spec, P()),
        out_specs=(spec,) * 4,
        check_vma=False,
    )
```
